32 devices in a mesh: gx: 4 (over y, x), gy: 8 (over z, core).
Axes of the slice: x: 2, y: 2, z: 4, core: 2. Of those that a mesh axis runs over, the one named last changes fastest.
Arguments:
- a_blocks: bfloat16 [16, 16, 5, 192, 192], P('gx', 'gy'), may hold values from -0.4375 to 0.4375
- a_codes: int32 [16, 16, 5], P('gx', 'gy'), may hold values from 0 to 9, as said below
- p_blocks: bfloat16 [16, 16, 3, 12, 192], P('gx', 'gy'), may hold values from -0.875 to 0.875
- p_codes: int32 [16, 16, 3], P('gx', 'gy'), may hold values from 0 to 5, as said below
Outputs:
- coarse: float32 [16, 16, 12, 588], P('gx', 'gy')
The draws below stay inside these ranges and needn't reach their ends.
Inputs may be any that keep to these rules, and one draw needn't show every extreme that they name: `a_codes`: slot 0 is 4 (the aggregate itself); the other slots of one aggregate hold distinct codes or 9; some aggregates have every slot live. `p_codes`: slot 0 is 0 (the aggregate itself); the other slots of one aggregate hold distinct codes of 1 to 4 or 5; some aggregates have every slot live.
All inputs are finite; a program needn't handle non-finite values.
Results may differ from the reference program's by a relative error of at most 0.0029.
Values may be sent and summed in bfloat16 or wider, within the bound.
No kernel may reach another device: no remote copies, remote signals or barrier semaphores. Data moves between devices by JAX's collectives and lax.ppermute only.
A program may use at most 64 MiB of HBM per device.

```python
import jax
import jax.numpy as jnp
import numpy as np
from jax import lax

F = 192
C = 12
KA = 5
KP = 3
AGX = 16
AGY = 16


def draw_a_codes(key, part):
    first_key, second_key = jax.random.split(jax.random.fold_in(key, 11))
    scores = jax.random.randint(first_key, (AGX, AGY, 8), 0, 1 << 20) * 8 + jnp.arange(8, dtype=jnp.int32)
    order = jnp.argsort(scores, axis=-1).astype(jnp.int32)
    neighbours = jnp.where(order >= 4, order + 1, order)[..., :KA - 1]
    keep = jax.random.randint(second_key, (AGX, AGY, KA - 1), 0, 4) > 0
    row_x = jnp.arange(AGX, dtype=jnp.int32)[:, None]
    row_y = jnp.arange(AGY, dtype=jnp.int32)[None, :]
    filled = ((row_x + row_y) % 3 == 0)[..., None]
    neighbours = jnp.where(keep | filled, neighbours, 9)
    itself = jnp.full((AGX, AGY, 1), 4, jnp.int32)
    return jnp.concatenate([itself, neighbours], axis=-1).astype(jnp.int32)


def draw_p_codes(key, part):
    first_key, second_key = jax.random.split(jax.random.fold_in(key, 23))
    scores = jax.random.randint(first_key, (AGX, AGY, 4), 0, 1 << 20) * 4 + jnp.arange(4, dtype=jnp.int32)
    order = jnp.argsort(scores, axis=-1).astype(jnp.int32)
    neighbours = (order + 1)[..., :KP - 1]
    keep = jax.random.randint(second_key, (AGX, AGY, KP - 1), 0, 4) > 0
    row_x = jnp.arange(AGX, dtype=jnp.int32)[:, None]
    row_y = jnp.arange(AGY, dtype=jnp.int32)[None, :]
    filled = ((row_x + 2 * row_y) % 3 == 0)[..., None]
    neighbours = jnp.where(keep | filled, neighbours, 5)
    itself = jnp.zeros((AGX, AGY, 1), jnp.int32)
    return jnp.concatenate([itself, neighbours], axis=-1).astype(jnp.int32)


def block_scale(own_key, shape, cuts, least, high):
    gain, own = 1.0, jax.random.fold_in(own_key, 6)
    for axis_at, blocks in cuts:
        steps = jnp.exp(jax.random.uniform(jax.random.fold_in(own, axis_at), (blocks,), jnp.float32, least / len(cuts), high / len(cuts)))
        gain = gain * jnp.repeat(steps, shape[axis_at] // blocks).reshape([-1 if axis == axis_at else 1 for axis in range(len(shape))])
    return gain


def noise(key, dims, width, most, cuts=(), kind=jnp.bfloat16):
    result = width * jax.random.normal(key, dims, jnp.float32)
    if cuts:
        result = result * block_scale(key, dims, cuts, -0.22, 0.18)
    return jnp.clip(result, -most, most).astype(kind)


def setup_inputs(seed: int = 0) -> dict:
    key_list = jax.random.split(jax.random.key(seed), 5)
    a_blocks = noise(key_list[0], (AGX, AGY, KA, F, F), F ** -0.5, 0.4375, ((0, 4), (1, 8)))
    a_codes = draw_a_codes(jax.random.fold_in(key_list[4], 71), 0)
    p_blocks = noise(key_list[2], (AGX, AGY, KP, C, F), (F // 4) ** -0.5, 0.875, ((0, 4), (1, 8)))
    p_codes = draw_p_codes(jax.random.fold_in(key_list[4], 71), 0)
    return {"a_blocks": a_blocks, "a_codes": a_codes, "p_blocks": p_blocks, "p_codes": p_codes}


near_steps = tuple((shift_x, shift_y) for shift_x in (-1, 0, 1) for shift_y in (-1, 0, 1))
face_steps = ((0, 0), (-1, 0), (1, 0), (0, -1), (0, 1))


def spread_table():
    table = np.zeros((9, 5, 25), np.float32)
    for near_index, (shift_x, shift_y) in enumerate(near_steps):
        for face_index, (face_x, face_y) in enumerate(face_steps):
            table[near_index, face_index, (shift_x + face_x + 2) * 5 + shift_y + face_y + 2] = 1.0
    return table


def row_products(a_rows, a_slots, near_blocks):
    amount = a_rows.shape[0]
    flat_near = near_blocks.reshape((9 * amount,) + near_blocks.shape[2:])
    spread = jnp.asarray(spread_table()).reshape(9, 125)
    summed = jnp.zeros((amount, 25) + near_blocks.shape[3:], jnp.float32)
    for slot_index in range(a_slots.shape[1]):
        slot_codes = a_slots[:, slot_index]
        picked = (jnp.minimum(slot_codes, 8) * amount + jnp.arange(amount, dtype=jnp.int32)).astype(jnp.int32)
        chosen = flat_near[picked]
        product = jnp.einsum("nqcj,nij->nqci", chosen.astype(jnp.float32), a_rows[:, slot_index].astype(jnp.float32),
                             precision=lax.Precision.HIGHEST)
        weights = jnp.dot(jax.nn.one_hot(slot_codes, 9, dtype=jnp.float32), spread,
                          precision=lax.Precision.HIGHEST).reshape(amount, 5, 25)
        summed = summed + jnp.einsum("nqo,nqci->noci", weights, product, precision=lax.Precision.HIGHEST)
    return summed.astype(jnp.bfloat16)


def coarse_part(face_rows, coupled, face_index):
    terms = jnp.einsum("nci,noei->ncoe", face_rows.astype(jnp.float32), coupled.astype(jnp.float32),
                       precision=lax.Precision.HIGHEST)
    amount, unknowns = terms.shape[0], terms.shape[1]
    face_x, face_y = face_steps[face_index]
    layout = terms.reshape(amount, unknowns, 5, 5, unknowns)
    layout = jnp.pad(layout, ((0, 0), (0, 0), (1 - face_x, 1 + face_x), (1 - face_y, 1 + face_y), (0, 0)))
    return layout.reshape(amount, unknowns, 49 * unknowns)


def reference(a_blocks, a_codes, p_blocks, p_codes):
    face_blocks = jnp.einsum("xymf,xymcj->xyfcj", jax.nn.one_hot(p_codes, 5, dtype=jnp.float32),
                             p_blocks.astype(jnp.float32), precision=lax.Precision.HIGHEST).astype(jnp.bfloat16)
    widths = ((1, 1), (1, 1), (0, 0), (0, 0), (0, 0))
    padded_faces = jnp.pad(face_blocks, widths)
    columns = face_blocks.shape[1]

    def first(row_index):
        window = lax.dynamic_slice_in_dim(padded_faces, row_index, 3, 0)
        near_blocks = jnp.stack([window[1 + shift_x, 1 + shift_y:1 + shift_y + columns] for shift_x, shift_y in near_steps])
        return row_products(a_blocks[row_index], a_codes[row_index], near_blocks)

    row_ids = jnp.arange(face_blocks.shape[0], dtype=jnp.int32)
    coupled = lax.map(first, row_ids)
    padded_coupled = jnp.pad(coupled, widths)

    def second(row_index):
        face_window = lax.dynamic_slice_in_dim(padded_faces, row_index, 3, 0)
        coupled_window = lax.dynamic_slice_in_dim(padded_coupled, row_index, 3, 0)
        summed = jnp.zeros((columns, C, 49 * C), jnp.float32)
        for face_index, (face_x, face_y) in enumerate(face_steps):
            face_rows = face_window[1 - face_x, 1 - face_y:1 - face_y + columns, face_index]
            coupled_rows = coupled_window[1 - face_x, 1 - face_y:1 - face_y + columns]
            summed = summed + coarse_part(face_rows, coupled_rows, face_index)
        return summed

    return lax.map(second, row_ids)
```

```python
import jax
import jax.numpy as jnp
from jax import lax
from jax.experimental import pallas as pl
from jax.experimental.pallas import tpu as pltpu
from jax.sharding import PartitionSpec as P

face_steps = ((0, 0), (-1, 0), (1, 0), (0, -1), (0, 1))
ROWS = 16
NT = (((1,), (1,)), ((), ()))
AXES = ("gx", "gy")


def exchange_pairs(count_x, count_y):
    spot = lambda x, y: x * count_y + y
    result = []
    for parity in (0, 1):
        pairs = []
        for x in range(count_x):
            other = x + 1 if (x % 2 == parity) else x - 1
            for y in range(count_y):
                inside = 0 <= other < count_x
                pairs.append((spot(x, y), spot(other, y) if inside else spot(x, y ^ 1)))
        result.append(pairs)
    for parity in (0, 1):
        pairs = []
        for y in range(count_y):
            other = y + 1 if (y % 2 == parity) else y - 1
            for x in range(count_x):
                inside = 0 <= other < count_y
                pairs.append((spot(x, y), spot(x, other) if inside else spot(x ^ 1, y)))
        result.append(pairs)
    return result


def place(axis):
    index = lax.axis_index(axis)
    even = lax.rem(index, 2) == 0
    return index, even


def vmem(count):
    return [pl.BlockSpec(memory_space=pltpu.VMEM)] * count


def call(body, inputs, outputs, scratch=(), smem=0, name=None):
    return pl.pallas_call(
        body,
        out_shape=outputs,
        in_specs=[pl.BlockSpec(memory_space=pltpu.SMEM)] * smem + vmem(len(inputs) - smem),
        out_specs=vmem(len(outputs)) if isinstance(outputs, (tuple, list)) else vmem(1)[0],
        scratch_shapes=list(scratch),
        name=name,
    )(*inputs)


def faces_kernel(codes, p_ref, faces, send_a, send_b):
    tile_x, tile_y, slots, unknowns, edges = p_ref.shape
    _, even = place("gx")
    faces[...] = jnp.zeros_like(faces)
    for x in range(tile_x):
        for y in range(tile_y):
            for m in range(slots):
                faces[x, y, codes[x, y, m], 0:unknowns, :] = p_ref[x, y, m]
    send_a[...] = faces[jnp.where(even, tile_x - 1, 0), :, 0:5]
    send_b[...] = faces[jnp.where(even, 0, tile_x - 1), :, 0:5]


def x_sides(got_a, got_b, count_x):
    index, even = place("gx")

    def lower(y):
        value = jnp.where(even, got_b[y], got_a[y])
        return jnp.where(index > 0, value, jnp.zeros_like(value))

    def upper(y):
        value = jnp.where(even, got_a[y], got_b[y])
        return jnp.where(index < count_x - 1, value, jnp.zeros_like(value))

    return lower, upper


def strips_kernel(count_x):
    def body(faces, got_a, got_b, send_a, send_b):
        tile_x, tile_y = faces.shape[:2]
        _, even = place("gy")
        lower, upper = x_sides(got_a, got_b, count_x)
        for send, column in (
            (send_a, jnp.where(even, tile_y - 1, 0)),
            (send_b, jnp.where(even, 0, tile_y - 1)),
        ):
            send[0] = lower(column)
            send[tile_x + 1] = upper(column)
            for x in range(tile_x):
                send[1 + x] = faces[x, column, 0:5]

    return body


def terms_kernel(count_x, count_y, unknowns):
    span = 49 * unknowns
    lanes = -(-span // 128) * 128

    def body(
        a_codes, a_ref, faces, got_xa, got_xb, got_ya, got_yb,
        own, send_xa, send_xb, send_ya, send_yb,
        near, summed, coupled, total, side_x, side_y,
    ):
        tile_x, tile_y, slots, edges, _ = a_ref.shape
        _, even_x = place("gx")
        index_y, even_y = place("gy")
        wide = tile_y + 2
        lower, upper = x_sides(got_xa, got_xb, count_x)
        blank = (tile_x + 2) * wide
        flat = (5 * ROWS, edges)
        near[blank] = jnp.zeros(flat, near.dtype)
        for y in range(tile_y):
            near[1 + y] = lower(y).reshape(flat)
            near[(tile_x + 1) * wide + 1 + y] = upper(y).reshape(flat)
            for x in range(tile_x):
                near[(1 + x) * wide + 1 + y] = faces[x, y, 0:5].reshape(flat)
        for x in range(tile_x + 2):
            left = jnp.where(even_y, got_yb[x], got_ya[x])
            left = jnp.where(index_y > 0, left, jnp.zeros_like(left))
            near[x * wide] = left.reshape(flat)
            right = jnp.where(even_y, got_ya[x], got_yb[x])
            right = jnp.where(index_y < count_y - 1, right, jnp.zeros_like(right))
            near[x * wide + wide - 1] = right.reshape(flat)
        coupled[...] = jnp.zeros_like(coupled)
        total[...] = jnp.zeros_like(total)
        for x in range(tile_x):
            for y in range(tile_y):
                rows = summed.at[(x * tile_y + y) % summed.shape[0]]
                rows[...] = jnp.zeros(rows.shape, rows.dtype)
                for k in range(slots):
                    code = a_codes[x, y, k]
                    live = code < 9
                    step_x = lax.div(code, 3)
                    step_y = lax.rem(code, 3)
                    spot = jnp.where(live, (x + step_x) * wide + y + step_y, blank)
                    base = jnp.where(live, (step_x + 1) * 5 + step_y + 1, 12)
                    product = lax.dot_general(
                        near[spot], a_ref[x, y, k], NT, preferred_element_type=jnp.float32
                    )
                    for q, (face_x, face_y) in enumerate(face_steps):
                        rows[base + face_x * 5 + face_y] += product[q * ROWS : (q + 1) * ROWS]
                stack = coupled.at[(x * tile_y + y) % coupled.shape[0]]
                for o in range(25):
                    row = ((o // 5 + 1) * 7 + o % 5 + 1) * unknowns
                    stack[row : row + unknowns, :] = rows[o, 0:unknowns, :]
                terms = lax.dot_general(
                    near[(1 + x) * wide + 1 + y],
                    stack[...].astype(jnp.bfloat16),
                    NT,
                    preferred_element_type=jnp.float32,
                )
                for q, (face_x, face_y) in enumerate(face_steps):
                    part = terms[q * ROWS : (q + 1) * ROWS]
                    shift = (face_x * 7 + face_y) * unknowns
                    if shift:
                        part = pltpu.roll(part, (-shift) % lanes, 1)
                    to_x, to_y = x + face_x, y + face_y
                    if to_x < 0 or to_x >= tile_x:
                        side_x[0 if to_x < 0 else 1, y] = part
                    elif to_y < 0 or to_y >= tile_y:
                        side_y[0 if to_y < 0 else 1, x] = part
                    else:
                        total[to_x, to_y] += part
        own[...] = total[:, :, 0:unknowns, 0:span]
        for send, side, pick in (
            (send_xa, side_x, jnp.where(even_x, 1, 0)),
            (send_xb, side_x, jnp.where(even_x, 0, 1)),
            (send_ya, side_y, jnp.where(even_y, 1, 0)),
            (send_yb, side_y, jnp.where(even_y, 0, 1)),
        ):
            send[...] = side[pick].astype(send.dtype)

    return body


def sum_kernel(count_x, count_y):
    def body(own, got_xa, got_xb, got_ya, got_yb, result):
        tile_x, tile_y, unknowns, span = own.shape
        index_x, even_x = place("gx")
        index_y, even_y = place("gy")

        def shown(value, live):
            value = value[0:unknowns, 0:span].astype(jnp.float32)
            return jnp.where(live, value, jnp.zeros_like(value))

        result[...] = own[...]
        low_x, high_x = index_x > 0, index_x < count_x - 1
        low_y, high_y = index_y > 0, index_y < count_y - 1
        for y in range(tile_y):
            result[0, y] += shown(jnp.where(even_x, got_xb[y], got_xa[y]), low_x)
            result[tile_x - 1, y] += shown(jnp.where(even_x, got_xa[y], got_xb[y]), high_x)
        for x in range(tile_x):
            result[x, 0] += shown(jnp.where(even_y, got_yb[x], got_ya[x]), low_y)
            result[x, tile_y - 1] += shown(jnp.where(even_y, got_ya[x], got_yb[x]), high_y)

    return body


def solution(mesh):
    count_x, count_y = mesh.shape["gx"], mesh.shape["gy"]
    pairs = exchange_pairs(count_x, count_y)

    def shards(a_blocks, a_codes, p_blocks, p_codes):
        tile_x, tile_y, slots, edges, _ = a_blocks.shape
        unknowns = p_blocks.shape[3]
        span = 49 * unknowns
        lanes = -(-span // 128) * 128
        half = lambda *dims: jax.ShapeDtypeStruct(dims, jnp.bfloat16)
        block = (5, ROWS, edges)
        faces, send_a, send_b = call(
            faces_kernel,
            (p_codes, p_blocks),
            (half(tile_x, tile_y, 6, ROWS, edges), half(tile_y, *block), half(tile_y, *block)),
            smem=1,
            name="faces",
        )
        got_xa = lax.ppermute(send_a, AXES, pairs[0])
        got_xb = lax.ppermute(send_b, AXES, pairs[1])
        send_a, send_b = call(
            strips_kernel(count_x),
            (faces, got_xa, got_xb),
            (half(tile_x + 2, *block), half(tile_x + 2, *block)),
            name="strips",
        )
        got_ya = lax.ppermute(send_a, AXES, pairs[2])
        got_yb = lax.ppermute(send_b, AXES, pairs[3])
        own, *sends = call(
            terms_kernel(count_x, count_y, unknowns),
            (a_codes, a_blocks, faces, got_xa, got_xb, got_ya, got_yb),
            (
                jax.ShapeDtypeStruct((tile_x, tile_y, unknowns, span), jnp.float32),
                half(tile_y, ROWS, lanes),
                half(tile_y, ROWS, lanes),
                half(tile_x, ROWS, lanes),
                half(tile_x, ROWS, lanes),
            ),
            scratch=(
                pltpu.VMEM(((tile_x + 2) * (tile_y + 2) + 1, 5 * ROWS, edges), jnp.bfloat16),
                pltpu.VMEM((2, 25, ROWS, edges), jnp.float32),
                pltpu.VMEM((2, lanes, edges), jnp.float32),
                pltpu.VMEM((tile_x, tile_y, ROWS, lanes), jnp.float32),
                pltpu.VMEM((2, tile_y, ROWS, lanes), jnp.float32),
                pltpu.VMEM((2, tile_x, ROWS, lanes), jnp.float32),
            ),
            smem=1,
            name="terms",
        )
        got = [lax.ppermute(send, AXES, p) for send, p in zip(sends, pairs)]
        return call(
            sum_kernel(count_x, count_y),
            (own, *got),
            jax.ShapeDtypeStruct((tile_x, tile_y, unknowns, span), jnp.float32),
            name="sum",
        )

    in_specs = (
        P("gx", "gy", None, None, None),
        P("gx", "gy", None),
        P("gx", "gy", None, None, None),
        P("gx", "gy", None),
    )
    out_specs = P("gx", "gy", None, None)
    return jax.shard_map(shards, mesh=mesh, in_specs=in_specs, out_specs=out_specs, check_vma=False)
```

```python
import jax
import jax.numpy as jnp
from jax import lax
from jax.experimental import pallas as pl
from jax.experimental.pallas import tpu as pltpu
from jax.sharding import PartitionSpec as P

face_steps = ((0, 0), (-1, 0), (1, 0), (0, -1), (0, 1))
ROWS = 16
NT = (((1,), (1,)), ((), ()))
AXES = ("gx", "gy")


def exchange_pairs(count_x, count_y):
    spot = lambda x, y: x * count_y + y
    result = []
    for parity in (0, 1):
        pairs = []
        for x in range(count_x):
            other = x + 1 if (x % 2 == parity) else x - 1
            for y in range(count_y):
                inside = 0 <= other < count_x
                pairs.append((spot(x, y), spot(other, y) if inside else spot(x, y ^ 1)))
        result.append(pairs)
    for parity in (0, 1):
        pairs = []
        for y in range(count_y):
            other = y + 1 if (y % 2 == parity) else y - 1
            for x in range(count_x):
                inside = 0 <= other < count_y
                pairs.append((spot(x, y), spot(x, other) if inside else spot(x ^ 1, y)))
        result.append(pairs)
    return result


def place(axis):
    index = lax.axis_index(axis)
    even = lax.rem(index, 2) == 0
    return index, even


def vmem(count):
    return [pl.BlockSpec(memory_space=pltpu.VMEM)] * count


def call(body, inputs, outputs, scratch=(), smem=0, name=None):
    return pl.pallas_call(
        body,
        out_shape=outputs,
        in_specs=[pl.BlockSpec(memory_space=pltpu.SMEM)] * smem + vmem(len(inputs) - smem),
        out_specs=vmem(len(outputs)) if isinstance(outputs, (tuple, list)) else vmem(1)[0],
        scratch_shapes=list(scratch),
        compiler_params=pltpu.CompilerParams(vmem_limit_bytes=20 << 20),
        name=name,
    )(*inputs)


def faces_kernel(codes, p_ref, faces, send_a, send_b):
    tile_x, slots, unknowns, tile_y, edges = p_ref.shape
    _, even = place("gx")
    faces[...] = jnp.zeros_like(faces)
    for x in range(tile_x):
        for m in range(slots):
            rows = p_ref[x, m]
            for y in range(tile_y):
                faces[x, y, codes[m, y, x], 0:unknowns, :] = rows[:, y, :]
    send_a[...] = faces[jnp.where(even, tile_x - 1, 0), :, 0:5]
    send_b[...] = faces[jnp.where(even, 0, tile_x - 1), :, 0:5]


def x_sides(got_a, got_b, count_x):
    index, even = place("gx")

    def lower(y):
        value = jnp.where(even, got_b[y], got_a[y])
        return jnp.where(index > 0, value, jnp.zeros_like(value))

    def upper(y):
        value = jnp.where(even, got_a[y], got_b[y])
        return jnp.where(index < count_x - 1, value, jnp.zeros_like(value))

    return lower, upper


def strips_kernel(count_x):
    def body(faces, got_a, got_b, send_a, send_b):
        tile_x, tile_y = faces.shape[:2]
        _, even = place("gy")
        lower, upper = x_sides(got_a, got_b, count_x)
        for send, column in (
            (send_a, jnp.where(even, tile_y - 1, 0)),
            (send_b, jnp.where(even, 0, tile_y - 1)),
        ):
            send[0] = lower(column)
            send[tile_x + 1] = upper(column)
            for x in range(tile_x):
                send[1 + x] = faces[x, column, 0:5]

    return body


def terms_kernel(count_x, count_y, unknowns):
    span = 49 * unknowns
    lanes = -(-span // 128) * 128

    def body(
        a_codes, a_ref, faces, got_xa, got_xb, got_ya, got_yb,
        own, send_xa, send_xb, send_ya, send_yb,
        near, summed, coupled, total, side_x, side_y,
    ):
        tile_x, tile_y, slots, edges, _ = a_ref.shape
        _, even_x = place("gx")
        index_y, even_y = place("gy")
        wide = tile_y + 2
        lower, upper = x_sides(got_xa, got_xb, count_x)
        blank = (tile_x + 2) * wide
        flat = (5 * ROWS, edges)
        near[blank] = jnp.zeros(flat, near.dtype)
        for y in range(tile_y):
            near[1 + y] = lower(y).reshape(flat)
            near[(tile_x + 1) * wide + 1 + y] = upper(y).reshape(flat)
            for x in range(tile_x):
                near[(1 + x) * wide + 1 + y] = faces[x, y, 0:5].reshape(flat)
        for x in range(tile_x + 2):
            left = jnp.where(even_y, got_yb[x], got_ya[x])
            left = jnp.where(index_y > 0, left, jnp.zeros_like(left))
            near[x * wide] = left.reshape(flat)
            right = jnp.where(even_y, got_ya[x], got_yb[x])
            right = jnp.where(index_y < count_y - 1, right, jnp.zeros_like(right))
            near[x * wide + wide - 1] = right.reshape(flat)
        coupled[...] = jnp.zeros_like(coupled)
        total[...] = jnp.zeros_like(total)
        for x in range(tile_x):
            for y in range(tile_y):
                rows = summed.at[(x * tile_y + y) % summed.shape[0]]
                rows[...] = jnp.zeros(rows.shape, rows.dtype)
                for k in range(slots):
                    code = a_codes[x, y, k]
                    live = code < 9
                    step_x = lax.div(code, 3)
                    step_y = lax.rem(code, 3)
                    spot = jnp.where(live, (x + step_x) * wide + y + step_y, blank)
                    base = jnp.where(live, (step_x + 1) * 5 + step_y + 1, 12)
                    product = lax.dot_general(
                        near[spot], a_ref[x, y, k], NT, preferred_element_type=jnp.float32
                    )
                    for q, (face_x, face_y) in enumerate(face_steps):
                        rows[base + face_x * 5 + face_y] += product[q * ROWS : (q + 1) * ROWS]
                stack = coupled.at[(x * tile_y + y) % coupled.shape[0]]
                for o in range(25):
                    row = ((o // 5 + 1) * 7 + o % 5 + 1) * unknowns
                    stack[row : row + unknowns, :] = rows[o, 0:unknowns, :]
                terms = lax.dot_general(
                    near[(1 + x) * wide + 1 + y],
                    stack[...].astype(jnp.bfloat16),
                    NT,
                    preferred_element_type=jnp.float32,
                )
                for q, (face_x, face_y) in enumerate(face_steps):
                    part = terms[q * ROWS : (q + 1) * ROWS]
                    shift = (face_x * 7 + face_y) * unknowns
                    if shift:
                        part = pltpu.roll(part, (-shift) % lanes, 1)
                    to_x, to_y = x + face_x, y + face_y
                    if to_x < 0 or to_x >= tile_x:
                        side_x[0 if to_x < 0 else 1, y] = part
                    elif to_y < 0 or to_y >= tile_y:
                        side_y[0 if to_y < 0 else 1, x] = part
                    else:
                        total[to_x, to_y] += part
        own[...] = total[:, :, 0:unknowns, 0:span]
        for send, side, pick in (
            (send_xa, side_x, jnp.where(even_x, 1, 0)),
            (send_xb, side_x, jnp.where(even_x, 0, 1)),
            (send_ya, side_y, jnp.where(even_y, 1, 0)),
            (send_yb, side_y, jnp.where(even_y, 0, 1)),
        ):
            send[...] = side[pick].astype(send.dtype)

    return body


def sum_kernel(count_x, count_y):
    def body(own, got_xa, got_xb, got_ya, got_yb, result):
        tile_x, tile_y, unknowns, span = own.shape
        index_x, even_x = place("gx")
        index_y, even_y = place("gy")

        def shown(value, live):
            value = value[0:unknowns, 0:span].astype(jnp.float32)
            return jnp.where(live, value, jnp.zeros_like(value))

        low_x, high_x = index_x > 0, index_x < count_x - 1
        low_y, high_y = index_y > 0, index_y < count_y - 1
        for x in range(tile_x):
            for y in range(tile_y):
                value = own[x, y]
                if x == 0:
                    value += shown(jnp.where(even_x, got_xb[y], got_xa[y]), low_x)
                if x == tile_x - 1:
                    value += shown(jnp.where(even_x, got_xa[y], got_xb[y]), high_x)
                if y == 0:
                    value += shown(jnp.where(even_y, got_yb[x], got_ya[x]), low_y)
                if y == tile_y - 1:
                    value += shown(jnp.where(even_y, got_ya[x], got_yb[x]), high_y)
                result[x, :, y, :] = value

    return body


def solution(mesh):
    count_x, count_y = mesh.shape["gx"], mesh.shape["gy"]
    pairs = exchange_pairs(count_x, count_y)

    def shards(a_blocks, a_codes, p_blocks, p_codes):
        tile_x, tile_y, slots, edges, _ = a_blocks.shape
        unknowns = p_blocks.shape[3]
        span = 49 * unknowns
        lanes = -(-span // 128) * 128
        half = lambda *dims: jax.ShapeDtypeStruct(dims, jnp.bfloat16)
        block = (5, ROWS, edges)
        faces, send_a, send_b = call(
            faces_kernel,
            (jnp.transpose(p_codes, (2, 1, 0)), jnp.transpose(p_blocks, (0, 2, 3, 1, 4))),
            (half(tile_x, tile_y, 6, ROWS, edges), half(tile_y, *block), half(tile_y, *block)),
            smem=1,
            name="faces",
        )
        got_xa = lax.ppermute(send_a, AXES, pairs[0])
        got_xb = lax.ppermute(send_b, AXES, pairs[1])
        send_a, send_b = call(
            strips_kernel(count_x),
            (faces, got_xa, got_xb),
            (half(tile_x + 2, *block), half(tile_x + 2, *block)),
            name="strips",
        )
        got_ya = lax.ppermute(send_a, AXES, pairs[2])
        got_yb = lax.ppermute(send_b, AXES, pairs[3])
        own, *sends = call(
            terms_kernel(count_x, count_y, unknowns),
            (a_codes, a_blocks, faces, got_xa, got_xb, got_ya, got_yb),
            (
                jax.ShapeDtypeStruct((tile_x, tile_y, unknowns, span), jnp.float32),
                half(tile_y, ROWS, lanes),
                half(tile_y, ROWS, lanes),
                half(tile_x, ROWS, lanes),
                half(tile_x, ROWS, lanes),
            ),
            scratch=(
                pltpu.VMEM(((tile_x + 2) * (tile_y + 2) + 1, 5 * ROWS, edges), jnp.bfloat16),
                pltpu.VMEM((2, 25, ROWS, edges), jnp.float32),
                pltpu.VMEM((2, lanes, edges), jnp.float32),
                pltpu.VMEM((tile_x, tile_y, ROWS, lanes), jnp.float32),
                pltpu.VMEM((2, tile_y, ROWS, lanes), jnp.float32),
                pltpu.VMEM((2, tile_x, ROWS, lanes), jnp.float32),
            ),
            smem=1,
            name="terms",
        )
        got = [lax.ppermute(send, AXES, p) for send, p in zip(sends, pairs)]
        result = call(
            sum_kernel(count_x, count_y),
            (own, *got),
            jax.ShapeDtypeStruct((tile_x, unknowns, tile_y, span), jnp.float32),
            name="sum",
        )
        return jnp.transpose(result, (0, 2, 1, 3))

    in_specs = (
        P("gx", "gy", None, None, None),
        P("gx", "gy", None),
        P("gx", "gy", None, None, None),
        P("gx", "gy", None),
    )
    out_specs = P("gx", "gy", None, None)
    return jax.shard_map(shards, mesh=mesh, in_specs=in_specs, out_specs=out_specs, check_vma=False)
```

```python
import jax
import jax.numpy as jnp
from jax import lax
from jax.experimental import pallas as pl
from jax.experimental.pallas import tpu as pltpu
from jax.sharding import PartitionSpec as P

face_steps = ((0, 0), (-1, 0), (1, 0), (0, -1), (0, 1))
ROWS = 16
NT = (((1,), (1,)), ((), ()))
AXES = ("gx", "gy")


def exchange_pairs(count_x, count_y):
    spot = lambda x, y: x * count_y + y
    result = []
    for parity in (0, 1):
        pairs = []
        for x in range(count_x):
            other = x + 1 if (x % 2 == parity) else x - 1
            for y in range(count_y):
                inside = 0 <= other < count_x
                pairs.append((spot(x, y), spot(other, y) if inside else spot(x, y ^ 1)))
        result.append(pairs)
    for parity in (0, 1):
        pairs = []
        for y in range(count_y):
            other = y + 1 if (y % 2 == parity) else y - 1
            for x in range(count_x):
                inside = 0 <= other < count_y
                pairs.append((spot(x, y), spot(x, other) if inside else spot(x ^ 1, y)))
        result.append(pairs)
    return result


def place(axis):
    index = lax.axis_index(axis)
    even = lax.rem(index, 2) == 0
    return index, even


def run(body, inputs, spaces, outputs, scratch=(), cost=None, name=None):
    many = isinstance(outputs, (tuple, list))
    inside = pl.BlockSpec(memory_space=pltpu.VMEM)
    return pl.pallas_call(
        body,
        out_shape=outputs,
        in_specs=[pl.BlockSpec(memory_space=space) for space in spaces],
        out_specs=[inside] * len(outputs) if many else inside,
        scratch_shapes=list(scratch),
        compiler_params=pltpu.CompilerParams(vmem_limit_bytes=20 << 20),
        cost_estimate=cost,
        name=name,
    )(*inputs)


def packed(first, second):
    return first[:, :128], second[:, :128], jnp.concatenate([first[:, 128:], second[:, 128:]], axis=1)


def unpacked(wire, spot):
    half = wire.shape[-1] // 2
    rest = wire[spot // 2, 2]
    rest = rest[:, half:] if spot % 2 else rest[:, :half]
    return jnp.concatenate([wire[spot // 2, spot % 2], rest], axis=1)


def send_pairs(send, values):
    for pair in range(len(values) // 2):
        for part, value in enumerate(packed(values[2 * pair], values[2 * pair + 1])):
            send[pair, part] = value


def slots_kernel(codes_hbm, p_hbm, slots_ref, faces, send_a, send_b, codes, p_ref, arrived):
    tile_x, slots, unknowns, tile_y, edges = p_ref.shape
    _, even = place("gx")
    copies = [
        pltpu.make_async_copy(codes_hbm, codes, arrived.at[0]),
        pltpu.make_async_copy(p_hbm, p_ref, arrived.at[1]),
    ]
    for copy in copies:
        copy.start()
    faces[...] = jnp.zeros_like(faces)
    for copy in copies:
        copy.wait()
    pad = lax.broadcasted_iota(jnp.int32, (ROWS - unknowns, edges), 0) + 1
    for x in range(tile_x):
        for m in range(slots):
            rows = p_ref[x, m]
            for y in range(tile_y):
                code = codes[m, y, x]
                block = rows[:, y, :]
                faces[x, y, code, 0:unknowns, :] = block
                marks = jnp.where(pad == code, 1.0, 0.0).astype(jnp.bfloat16)
                slots_ref[x, y, m * ROWS : m * ROWS + unknowns, :] = block
                slots_ref[x, y, m * ROWS + unknowns : (m + 1) * ROWS, :] = marks
    for send, row in (
        (send_a, jnp.where(even, tile_x - 1, 0)),
        (send_b, jnp.where(even, 0, tile_x - 1)),
    ):
        send_pairs(send, [slots_ref[row, y] for y in range(tile_y)])


def x_side(got_a, got_b, y, even):
    from_a, from_b = unpacked(got_a, y), unpacked(got_b, y)
    return jnp.where(even, from_b, from_a), jnp.where(even, from_a, from_b)


def strips_kernel(slots_ref, got_a, got_b, send_a, send_b):
    tile_x, tile_y = slots_ref.shape[:2]
    _, even_x = place("gx")
    _, even_y = place("gy")
    first = x_side(got_a, got_b, 0, even_x)
    last = x_side(got_a, got_b, tile_y - 1, even_x)
    for send, upper in ((send_a, even_y), (send_b, jnp.logical_not(even_y))):
        column = jnp.where(upper, tile_y - 1, 0)
        ends = [jnp.where(upper, high, low) for low, high in zip(first, last)]
        middle = [slots_ref[x, column] for x in range(tile_x)]
        send_pairs(send, [ends[0], *middle, ends[1]])


def rows_kernel(slots_ref, a_hbm, result, a_ref, arrived):
    tile_x, tile_y, count = a_hbm.shape[:3]
    copies = {}
    for x in range(tile_x):
        for y in range(tile_y):
            copies[x, y] = pltpu.make_async_copy(
                a_hbm.at[x, y], a_ref.at[x, y], arrived.at[x * tile_y + y]
            )
            copies[x, y].start()
    for x in range(tile_x):
        for y in range(tile_y):
            copies[x, y].wait()
            for k in range(count):
                result[x, y, k] = jnp.dot(
                    slots_ref[x, y], a_ref[x, y, k], preferred_element_type=jnp.float32
                ).astype(result.dtype)


def terms_kernel(count_x, count_y, unknowns):
    span = 49 * unknowns
    lanes = -(-span // 128) * 128

    def body(
        a_hbm, p_hbm, u_ref, faces, got_xa, got_xb, got_ya, got_yb,
        own, send_xa, send_xb, send_ya, send_yb,
        a_codes, p_codes, near, summed, spread, total, arrived,
    ):
        tile_x, tile_y, slots, held, edges = u_ref.shape
        copies = [
            pltpu.make_async_copy(a_hbm, a_codes, arrived.at[0]),
            pltpu.make_async_copy(p_hbm, p_codes, arrived.at[1]),
        ]
        for copy in copies:
            copy.start()
        index_x, even_x = place("gx")
        index_y, even_y = place("gy")
        wide = tile_y + 2
        blank = (tile_x + 2) * wide
        near[blank] = jnp.zeros(near.shape[1:], near.dtype)

        def expand(spot, value, live):
            value = jnp.where(live, value, jnp.zeros_like(value))
            near[spot, 0:ROWS, :] = value[0:ROWS]
            for q in range(1, 5):
                block = jnp.zeros((ROWS, edges), near.dtype)
                for m in range(1, held // ROWS):
                    mark = value[m * ROWS + unknowns + q - 1 : m * ROWS + unknowns + q]
                    block += mark * value[m * ROWS : (m + 1) * ROWS]
                near[spot, q * ROWS : (q + 1) * ROWS, :] = block

        for y in range(tile_y):
            low, high = x_side(got_xa, got_xb, y, even_x)
            expand(1 + y, low, index_x > 0)
            expand((tile_x + 1) * wide + 1 + y, high, index_x < count_x - 1)
            for x in range(tile_x):
                near[(1 + x) * wide + 1 + y] = faces[x, y, 0:5].reshape(near.shape[1:])
        for x in range(tile_x + 2):
            from_a, from_b = unpacked(got_ya, x), unpacked(got_yb, x)
            inside = True
            if x == 0:
                inside = index_x > 0
            if x == tile_x + 1:
                inside = index_x < count_x - 1
            low, high = index_y > 0, index_y < count_y - 1
            expand(x * wide, jnp.where(even_y, from_b, from_a), jnp.logical_and(low, inside))
            expand(
                x * wide + wide - 1, jnp.where(even_y, from_a, from_b), jnp.logical_and(high, inside)
            )
        total[...] = jnp.zeros_like(total)
        spread[...] = jnp.zeros_like(spread)
        wing = lax.broadcasted_iota(jnp.int32, (ROWS, 128), 1) < 64
        row = lax.broadcasted_iota(jnp.int32, (held, 128), 0)
        lane = lax.broadcasted_iota(jnp.int32, (held, 128), 1)
        picks = jnp.where(jnp.logical_or(lane == row, lane == row + 64), 1.0, 0.0)
        picks = picks.astype(jnp.bfloat16)
        for copy in copies:
            copy.wait()
        for x in range(tile_x):
            for y in range(tile_y):
                turn = x * tile_y + y
                blocks = summed.at[turn % summed.shape[0]]
                blocks[...] = jnp.zeros(blocks.shape, blocks.dtype)
                for k in range(slots):
                    code = a_codes[x, y, k]
                    live = code < 9
                    step_x = lax.div(code, 3)
                    step_y = lax.rem(code, 3)
                    spot = jnp.where(live, (x + step_x) * wide + y + step_y, blank)
                    base = jnp.where(live, (step_x + 1) * 5 + step_y + 1, 12)
                    one = jnp.concatenate(
                        [u_ref[x, y, k], jnp.zeros((64 - held, edges), u_ref.dtype)], axis=0
                    )
                    product = lax.dot_general(
                        near[spot],
                        jnp.concatenate([one, one], axis=0),
                        NT,
                        preferred_element_type=jnp.float32,
                    )
                    for q, (face_x, face_y) in enumerate(face_steps):
                        blocks[base + face_x * 5 + face_y] += product[q * ROWS : (q + 1) * ROWS]
                stack = spread.at[turn % spread.shape[0]]
                for o in range(25):
                    value = blocks[o]
                    high = value.astype(jnp.bfloat16).astype(jnp.float32)
                    start = ((o // 5 + 1) * 7 + o % 5 + 1) * unknowns
                    stack[start : start + unknowns, :] = jnp.where(wing, high, value - high)[:unknowns]
                terms = lax.dot_general(
                    picks, stack[...].astype(jnp.bfloat16), NT, preferred_element_type=jnp.float32
                )
                for m in range(held // ROWS):
                    part = terms[m * ROWS : (m + 1) * ROWS]
                    spot = (1 + x) * wide + 1 + y
                    if m:
                        code = p_codes[m, y, x]
                        face_x = jnp.where(code == 1, -1, jnp.where(code == 2, 1, 0))
                        face_y = jnp.where(code == 3, -1, jnp.where(code == 4, 1, 0))
                        shift = (face_x * 7 + face_y) * unknowns
                        part = pltpu.roll(part, jnp.where(shift > 0, lanes - shift, -shift), 1)
                        spot = jnp.where(code < 5, spot + face_x * wide + face_y, blank)
                    total[spot] += part
        for x in range(tile_x):
            for y in range(tile_y):
                own[x, y] = total[(1 + x) * wide + 1 + y, 0:unknowns, 0:span]
        for send, far in ((send_xa, even_x), (send_xb, jnp.logical_not(even_x))):
            for y in range(tile_y):
                spot = jnp.where(far, (tile_x + 1) * wide, 0) + 1 + y
                send[y] = total[spot].astype(send.dtype)
        for send, far in ((send_ya, even_y), (send_yb, jnp.logical_not(even_y))):
            for x in range(tile_x):
                spot = (1 + x) * wide + jnp.where(far, wide - 1, 0)
                send[x] = total[spot].astype(send.dtype)

    return body


def sum_kernel(count_x, count_y):
    def body(own, got_xa, got_xb, got_ya, got_yb, result):
        tile_x, tile_y, unknowns, span = own.shape
        index_x, even_x = place("gx")
        index_y, even_y = place("gy")

        def shown(value, live):
            value = value[0:unknowns, 0:span].astype(jnp.float32)
            return jnp.where(live, value, jnp.zeros_like(value))

        low_x, high_x = index_x > 0, index_x < count_x - 1
        low_y, high_y = index_y > 0, index_y < count_y - 1
        for x in range(tile_x):
            for y in range(tile_y):
                value = own[x, y]
                if x == 0:
                    value += shown(jnp.where(even_x, got_xb[y], got_xa[y]), low_x)
                if x == tile_x - 1:
                    value += shown(jnp.where(even_x, got_xa[y], got_xb[y]), high_x)
                if y == 0:
                    value += shown(jnp.where(even_y, got_yb[x], got_ya[x]), low_y)
                if y == tile_y - 1:
                    value += shown(jnp.where(even_y, got_ya[x], got_yb[x]), high_y)
                result[x, :, y, :] = value

    return body


def solution(mesh):
    count_x, count_y = mesh.shape["gx"], mesh.shape["gy"]
    pairs = exchange_pairs(count_x, count_y)
    hbm, inside = pltpu.HBM, pltpu.VMEM

    def shards(a_blocks, a_codes, p_blocks, p_codes):
        tile_x, tile_y, slots, edges, _ = a_blocks.shape
        held, unknowns = p_blocks.shape[2:4]
        span = 49 * unknowns
        lanes = -(-span // 128) * 128
        half = lambda *dims: jax.ShapeDtypeStruct(dims, jnp.bfloat16)
        codes = jnp.transpose(p_codes, (2, 1, 0))
        blocks = jnp.transpose(p_blocks, (0, 2, 3, 1, 4))
        wire = (3, held * ROWS, 128)
        dma = pltpu.SemaphoreType.DMA
        slots_ref, faces, send_a, send_b = run(
            slots_kernel,
            (codes, blocks),
            (hbm, hbm),
            (
                half(tile_x, tile_y, held * ROWS, edges),
                half(tile_x, tile_y, 6, ROWS, edges),
                half(tile_y // 2, *wire),
                half(tile_y // 2, *wire),
            ),
            scratch=(
                pltpu.SMEM(codes.shape, codes.dtype),
                pltpu.VMEM(blocks.shape, blocks.dtype),
                dma((2,)),
            ),
            name="slots",
        )
        got_xa = lax.ppermute(send_a, AXES, pairs[0])
        got_xb = lax.ppermute(send_b, AXES, pairs[1])
        u_rows = run(
            rows_kernel,
            (slots_ref, a_blocks),
            (inside, hbm),
            half(tile_x, tile_y, slots, held * ROWS, edges),
            scratch=(pltpu.VMEM(a_blocks.shape, a_blocks.dtype), dma((tile_x * tile_y,))),
            cost=pl.CostEstimate(
                flops=2 * held * ROWS * a_blocks.size,
                bytes_accessed=2 * a_blocks.size,
                transcendentals=0,
            ),
            name="rows",
        )
        send_a, send_b = run(
            strips_kernel,
            (slots_ref, got_xa, got_xb),
            (inside,) * 3,
            (half(tile_x // 2 + 1, *wire), half(tile_x // 2 + 1, *wire)),
            name="strips",
        )
        got_ya = lax.ppermute(send_a, AXES, pairs[2])
        got_yb = lax.ppermute(send_b, AXES, pairs[3])
        ring = (tile_x + 2) * (tile_y + 2) + 1
        own, *sends = run(
            terms_kernel(count_x, count_y, unknowns),
            (a_codes, codes, u_rows, faces, got_xa, got_xb, got_ya, got_yb),
            (hbm, hbm) + (inside,) * 6,
            (
                jax.ShapeDtypeStruct((tile_x, tile_y, unknowns, span), jnp.float32),
                half(tile_y, ROWS, lanes),
                half(tile_y, ROWS, lanes),
                half(tile_x, ROWS, lanes),
                half(tile_x, ROWS, lanes),
            ),
            scratch=(
                pltpu.SMEM(a_codes.shape, a_codes.dtype),
                pltpu.SMEM(codes.shape, codes.dtype),
                pltpu.VMEM((ring, 5 * ROWS, edges), jnp.bfloat16),
                pltpu.VMEM((2, 25, ROWS, 128), jnp.float32),
                pltpu.VMEM((2, lanes, 128), jnp.float32),
                pltpu.VMEM((ring, ROWS, lanes), jnp.float32),
                dma((2,)),
            ),
            name="terms",
        )
        got = [lax.ppermute(send, AXES, p) for send, p in zip(sends, pairs)]
        result = run(
            sum_kernel(count_x, count_y),
            (own, *got),
            (inside,) * 5,
            jax.ShapeDtypeStruct((tile_x, unknowns, tile_y, span), jnp.float32),
            name="sum",
        )
        return jnp.transpose(result, (0, 2, 1, 3))

    in_specs = (
        P("gx", "gy", None, None, None),
        P("gx", "gy", None),
        P("gx", "gy", None, None, None),
        P("gx", "gy", None),
    )
    out_specs = P("gx", "gy", None, None)
    return jax.shard_map(shards, mesh=mesh, in_specs=in_specs, out_specs=out_specs, check_vma=False)
```

```python
import jax
import jax.numpy as jnp
from jax import lax
from jax.experimental import pallas as pl
from jax.experimental.pallas import tpu as pltpu
from jax.sharding import PartitionSpec as P

face_steps = ((0, 0), (-1, 0), (1, 0), (0, -1), (0, 1))
ROWS = 16
NT = (((1,), (1,)), ((), ()))
AXES = ("gx", "gy")


def exchange_pairs(count_x, count_y):
    spot = lambda x, y: x * count_y + y
    result = []
    for parity in (0, 1):
        pairs = []
        for x in range(count_x):
            other = x + 1 if (x % 2 == parity) else x - 1
            for y in range(count_y):
                inside = 0 <= other < count_x
                pairs.append((spot(x, y), spot(other, y) if inside else spot(x, y ^ 1)))
        result.append(pairs)
    for parity in (0, 1):
        pairs = []
        for y in range(count_y):
            other = y + 1 if (y % 2 == parity) else y - 1
            for x in range(count_x):
                inside = 0 <= other < count_y
                pairs.append((spot(x, y), spot(x, other) if inside else spot(x ^ 1, y)))
        result.append(pairs)
    return result


def place(axis):
    index = lax.axis_index(axis)
    even = lax.rem(index, 2) == 0
    return index, even


def run(body, inputs, spaces, outputs, scratch=(), cost=None, name=None):
    many = isinstance(outputs, (tuple, list))
    inside = pl.BlockSpec(memory_space=pltpu.VMEM)
    held = [
        pltpu.with_memory_space_constraint(value, space) if space == pltpu.HBM else value
        for value, space in zip(inputs, spaces)
    ]
    return pl.pallas_call(
        body,
        out_shape=outputs,
        in_specs=[pl.BlockSpec(memory_space=space) for space in spaces],
        out_specs=[inside] * len(outputs) if many else inside,
        scratch_shapes=list(scratch),
        compiler_params=pltpu.CompilerParams(vmem_limit_bytes=20 << 20),
        cost_estimate=cost,
        name=name,
    )(*held)


def packed(first, second):
    return first[:, :128], second[:, :128], jnp.concatenate([first[:, 128:], second[:, 128:]], axis=1)


def unpacked(wire, spot):
    half = wire.shape[-1] // 2
    rest = wire[spot // 2, 2]
    rest = rest[:, half:] if spot % 2 else rest[:, :half]
    return jnp.concatenate([wire[spot // 2, spot % 2], rest], axis=1)


def send_pairs(send, values):
    for pair in range(len(values) // 2):
        for part, value in enumerate(packed(values[2 * pair], values[2 * pair + 1])):
            send[pair, part] = value


def slots_kernel(codes_hbm, p_hbm, slots_ref, faces, send_a, send_b, codes, p_ref, arrived):
    tile_x, slots, unknowns, tile_y, edges = p_ref.shape
    _, even = place("gx")
    copies = [
        pltpu.make_async_copy(codes_hbm, codes, arrived.at[0]),
        pltpu.make_async_copy(p_hbm, p_ref, arrived.at[1]),
    ]
    for copy in copies:
        copy.start()
    faces[...] = jnp.zeros_like(faces)
    for copy in copies:
        copy.wait()
    pad = lax.broadcasted_iota(jnp.int32, (ROWS - unknowns, edges), 0) + 1
    for x in range(tile_x):
        for m in range(slots):
            rows = p_ref[x, m]
            for y in range(tile_y):
                code = codes[m, y, x]
                block = rows[:, y, :]
                faces[x, y, code, 0:unknowns, :] = block
                marks = jnp.where(pad == code, 1.0, 0.0).astype(jnp.bfloat16)
                slots_ref[x, y, m * ROWS : m * ROWS + unknowns, :] = block
                slots_ref[x, y, m * ROWS + unknowns : (m + 1) * ROWS, :] = marks
    for send, row in (
        (send_a, jnp.where(even, tile_x - 1, 0)),
        (send_b, jnp.where(even, 0, tile_x - 1)),
    ):
        send_pairs(send, [slots_ref[row, y] for y in range(tile_y)])


def x_side(got_a, got_b, y, even):
    from_a, from_b = unpacked(got_a, y), unpacked(got_b, y)
    return jnp.where(even, from_b, from_a), jnp.where(even, from_a, from_b)


def strips_kernel(slots_ref, got_a, got_b, send_a, send_b):
    tile_x, tile_y = slots_ref.shape[:2]
    _, even_x = place("gx")
    _, even_y = place("gy")
    first = x_side(got_a, got_b, 0, even_x)
    last = x_side(got_a, got_b, tile_y - 1, even_x)
    for send, upper in ((send_a, even_y), (send_b, jnp.logical_not(even_y))):
        column = jnp.where(upper, tile_y - 1, 0)
        ends = [jnp.where(upper, high, low) for low, high in zip(first, last)]
        middle = [slots_ref[x, column] for x in range(tile_x)]
        send_pairs(send, [ends[0], *middle, ends[1]])


def rows_kernel(slots_ref, a_hbm, result, a_ref, arrived):
    tile_x, tile_y, count = a_hbm.shape[:3]
    copies = {}
    for x in range(tile_x):
        for y in range(tile_y):
            copies[x, y] = pltpu.make_async_copy(
                a_hbm.at[x, y], a_ref.at[x, y], arrived.at[x * tile_y + y]
            )
            copies[x, y].start()
    for x in range(tile_x):
        for y in range(tile_y):
            copies[x, y].wait()
            for k in range(count):
                result[x, y, k] = jnp.dot(
                    slots_ref[x, y], a_ref[x, y, k], preferred_element_type=jnp.float32
                ).astype(result.dtype)


def terms_kernel(count_x, count_y, unknowns):
    span = 49 * unknowns
    lanes = -(-span // 128) * 128

    def body(
        a_hbm, p_hbm, u_ref, faces, got_xa, got_xb, got_ya, got_yb,
        own, send_xa, send_xb, send_ya, send_yb,
        a_codes, p_codes, near, summed, spread, total, arrived,
    ):
        tile_x, tile_y, slots, held, edges = u_ref.shape
        copies = [
            pltpu.make_async_copy(a_hbm, a_codes, arrived.at[0]),
            pltpu.make_async_copy(p_hbm, p_codes, arrived.at[1]),
        ]
        for copy in copies:
            copy.start()
        index_x, even_x = place("gx")
        index_y, even_y = place("gy")
        wide = tile_y + 2
        blank = (tile_x + 2) * wide
        near[blank] = jnp.zeros(near.shape[1:], near.dtype)

        def expand(spot, value, live):
            value = jnp.where(live, value, jnp.zeros_like(value))
            near[spot, 0:ROWS, :] = value[0:ROWS]
            for q in range(1, 5):
                block = jnp.zeros((ROWS, edges), near.dtype)
                for m in range(1, held // ROWS):
                    mark = value[m * ROWS + unknowns + q - 1 : m * ROWS + unknowns + q]
                    block += mark * value[m * ROWS : (m + 1) * ROWS]
                near[spot, q * ROWS : (q + 1) * ROWS, :] = block

        for y in range(tile_y):
            low, high = x_side(got_xa, got_xb, y, even_x)
            expand(1 + y, low, index_x > 0)
            expand((tile_x + 1) * wide + 1 + y, high, index_x < count_x - 1)
            for x in range(tile_x):
                near[(1 + x) * wide + 1 + y] = faces[x, y, 0:5].reshape(near.shape[1:])
        for x in range(tile_x + 2):
            from_a, from_b = unpacked(got_ya, x), unpacked(got_yb, x)
            inside = True
            if x == 0:
                inside = index_x > 0
            if x == tile_x + 1:
                inside = index_x < count_x - 1
            low, high = index_y > 0, index_y < count_y - 1
            expand(x * wide, jnp.where(even_y, from_b, from_a), jnp.logical_and(low, inside))
            expand(
                x * wide + wide - 1, jnp.where(even_y, from_a, from_b), jnp.logical_and(high, inside)
            )
        total[...] = jnp.zeros_like(total)
        spread[...] = jnp.zeros_like(spread)
        wing = lax.broadcasted_iota(jnp.int32, (ROWS, 128), 1) < 64
        row = lax.broadcasted_iota(jnp.int32, (held, 128), 0)
        lane = lax.broadcasted_iota(jnp.int32, (held, 128), 1)
        picks = jnp.where(jnp.logical_or(lane == row, lane == row + 64), 1.0, 0.0)
        picks = picks.astype(jnp.bfloat16)
        for copy in copies:
            copy.wait()
        for x in range(tile_x):
            for y in range(tile_y):
                turn = x * tile_y + y
                blocks = summed.at[turn % summed.shape[0]]
                blocks[...] = jnp.zeros(blocks.shape, blocks.dtype)
                for k in range(slots):
                    code = a_codes[x, y, k]
                    live = code < 9
                    step_x = lax.div(code, 3)
                    step_y = lax.rem(code, 3)
                    spot = jnp.where(live, (x + step_x) * wide + y + step_y, blank)
                    base = jnp.where(live, (step_x + 1) * 5 + step_y + 1, 12)
                    one = jnp.concatenate(
                        [u_ref[x, y, k], jnp.zeros((64 - held, edges), u_ref.dtype)], axis=0
                    )
                    product = lax.dot_general(
                        near[spot],
                        jnp.concatenate([one, one], axis=0),
                        NT,
                        preferred_element_type=jnp.float32,
                    )
                    for q, (face_x, face_y) in enumerate(face_steps):
                        blocks[base + face_x * 5 + face_y] += product[q * ROWS : (q + 1) * ROWS]
                stack = spread.at[turn % spread.shape[0]]
                for o in range(25):
                    value = blocks[o]
                    high = value.astype(jnp.bfloat16).astype(jnp.float32)
                    start = ((o // 5 + 1) * 7 + o % 5 + 1) * unknowns
                    stack[start : start + unknowns, :] = jnp.where(wing, high, value - high)[:unknowns]
                terms = lax.dot_general(
                    picks, stack[...].astype(jnp.bfloat16), NT, preferred_element_type=jnp.float32
                )
                for m in range(held // ROWS):
                    part = terms[m * ROWS : (m + 1) * ROWS]
                    spot = (1 + x) * wide + 1 + y
                    if m:
                        code = p_codes[m, y, x]
                        face_x = jnp.where(code == 1, -1, jnp.where(code == 2, 1, 0))
                        face_y = jnp.where(code == 3, -1, jnp.where(code == 4, 1, 0))
                        shift = (face_x * 7 + face_y) * unknowns
                        part = pltpu.roll(part, jnp.where(shift > 0, lanes - shift, -shift), 1)
                        spot = jnp.where(code < 5, spot + face_x * wide + face_y, blank)
                    total[spot] += part
        for x in range(tile_x):
            for y in range(tile_y):
                own[x, y] = total[(1 + x) * wide + 1 + y, 0:unknowns, 0:span]
        for send, far in ((send_xa, even_x), (send_xb, jnp.logical_not(even_x))):
            for y in range(tile_y):
                spot = jnp.where(far, (tile_x + 1) * wide, 0) + 1 + y
                send[y] = total[spot].astype(send.dtype)
        for send, far in ((send_ya, even_y), (send_yb, jnp.logical_not(even_y))):
            for x in range(tile_x):
                spot = (1 + x) * wide + jnp.where(far, wide - 1, 0)
                send[x] = total[spot].astype(send.dtype)

    return body


def sum_kernel(count_x, count_y):
    def body(own, got_xa, got_xb, got_ya, got_yb, result):
        tile_x, tile_y, unknowns, span = own.shape
        index_x, even_x = place("gx")
        index_y, even_y = place("gy")

        def shown(value, live):
            value = value[0:unknowns, 0:span].astype(jnp.float32)
            return jnp.where(live, value, jnp.zeros_like(value))

        low_x, high_x = index_x > 0, index_x < count_x - 1
        low_y, high_y = index_y > 0, index_y < count_y - 1
        for x in range(tile_x):
            for y in range(tile_y):
                value = own[x, y]
                if x == 0:
                    value += shown(jnp.where(even_x, got_xb[y], got_xa[y]), low_x)
                if x == tile_x - 1:
                    value += shown(jnp.where(even_x, got_xa[y], got_xb[y]), high_x)
                if y == 0:
                    value += shown(jnp.where(even_y, got_yb[x], got_ya[x]), low_y)
                if y == tile_y - 1:
                    value += shown(jnp.where(even_y, got_ya[x], got_yb[x]), high_y)
                result[x, :, y, :] = value

    return body


def solution(mesh):
    count_x, count_y = mesh.shape["gx"], mesh.shape["gy"]
    pairs = exchange_pairs(count_x, count_y)
    hbm, inside = pltpu.HBM, pltpu.VMEM

    def shards(a_blocks, a_codes, p_blocks, p_codes):
        tile_x, tile_y, slots, edges, _ = a_blocks.shape
        held, unknowns = p_blocks.shape[2:4]
        span = 49 * unknowns
        lanes = -(-span // 128) * 128
        half = lambda *dims: jax.ShapeDtypeStruct(dims, jnp.bfloat16)
        codes = jnp.transpose(p_codes, (2, 1, 0))
        blocks = jnp.transpose(p_blocks, (0, 2, 3, 1, 4))
        wire = (3, held * ROWS, 128)
        dma = pltpu.SemaphoreType.DMA
        slots_ref, faces, send_a, send_b = run(
            slots_kernel,
            (codes, blocks),
            (hbm, hbm),
            (
                half(tile_x, tile_y, held * ROWS, edges),
                half(tile_x, tile_y, 6, ROWS, edges),
                half(tile_y // 2, *wire),
                half(tile_y // 2, *wire),
            ),
            scratch=(
                pltpu.SMEM(codes.shape, codes.dtype),
                pltpu.VMEM(blocks.shape, blocks.dtype),
                dma((2,)),
            ),
            name="slots",
        )
        got_xa = lax.ppermute(send_a, AXES, pairs[0])
        got_xb = lax.ppermute(send_b, AXES, pairs[1])
        u_rows = run(
            rows_kernel,
            (slots_ref, a_blocks),
            (inside, hbm),
            half(tile_x, tile_y, slots, held * ROWS, edges),
            scratch=(pltpu.VMEM(a_blocks.shape, a_blocks.dtype), dma((tile_x * tile_y,))),
            cost=pl.CostEstimate(
                flops=2 * held * ROWS * a_blocks.size,
                bytes_accessed=2 * a_blocks.size,
                transcendentals=0,
            ),
            name="rows",
        )
        send_a, send_b = run(
            strips_kernel,
            (slots_ref, got_xa, got_xb),
            (inside,) * 3,
            (half(tile_x // 2 + 1, *wire), half(tile_x // 2 + 1, *wire)),
            name="strips",
        )
        got_ya = lax.ppermute(send_a, AXES, pairs[2])
        got_yb = lax.ppermute(send_b, AXES, pairs[3])
        ring = (tile_x + 2) * (tile_y + 2) + 1
        own, *sends = run(
            terms_kernel(count_x, count_y, unknowns),
            (a_codes, codes, u_rows, faces, got_xa, got_xb, got_ya, got_yb),
            (hbm, hbm) + (inside,) * 6,
            (
                jax.ShapeDtypeStruct((tile_x, tile_y, unknowns, span), jnp.float32),
                half(tile_y, ROWS, lanes),
                half(tile_y, ROWS, lanes),
                half(tile_x, ROWS, lanes),
                half(tile_x, ROWS, lanes),
            ),
            scratch=(
                pltpu.SMEM(a_codes.shape, a_codes.dtype),
                pltpu.SMEM(codes.shape, codes.dtype),
                pltpu.VMEM((ring, 5 * ROWS, edges), jnp.bfloat16),
                pltpu.VMEM((2, 25, ROWS, 128), jnp.float32),
                pltpu.VMEM((2, lanes, 128), jnp.float32),
                pltpu.VMEM((ring, ROWS, lanes), jnp.float32),
                dma((2,)),
            ),
            name="terms",
        )
        got = [lax.ppermute(send, AXES, p) for send, p in zip(sends, pairs)]
        result = run(
            sum_kernel(count_x, count_y),
            (own, *got),
            (inside,) * 5,
            jax.ShapeDtypeStruct((tile_x, unknowns, tile_y, span), jnp.float32),
            name="sum",
        )
        return jnp.transpose(result, (0, 2, 1, 3))

    in_specs = (
        P("gx", "gy", None, None, None),
        P("gx", "gy", None),
        P("gx", "gy", None, None, None),
        P("gx", "gy", None),
    )
    out_specs = P("gx", "gy", None, None)
    return jax.shard_map(shards, mesh=mesh, in_specs=in_specs, out_specs=out_specs, check_vma=False)
```

```python
import jax
import jax.numpy as jnp
from jax import lax
from jax.experimental import pallas as pl
from jax.experimental.pallas import tpu as pltpu
from jax.sharding import PartitionSpec as P

face_steps = ((0, 0), (-1, 0), (1, 0), (0, -1), (0, 1))
ROWS = 16
NT = (((1,), (1,)), ((), ()))
AXES = ("gx", "gy")


def exchange_pairs(count_x, count_y):
    spot = lambda x, y: x * count_y + y
    result = []
    for parity in (0, 1):
        pairs = []
        for x in range(count_x):
            other = x + 1 if (x % 2 == parity) else x - 1
            for y in range(count_y):
                inside = 0 <= other < count_x
                pairs.append((spot(x, y), spot(other, y) if inside else spot(x, y ^ 1)))
        result.append(pairs)
    for parity in (0, 1):
        pairs = []
        for y in range(count_y):
            other = y + 1 if (y % 2 == parity) else y - 1
            for x in range(count_x):
                inside = 0 <= other < count_y
                pairs.append((spot(x, y), spot(x, other) if inside else spot(x ^ 1, y)))
        result.append(pairs)
    return result


def place(axis):
    index = lax.axis_index(axis)
    even = lax.rem(index, 2) == 0
    return index, even


def run(body, inputs, spaces, outputs, scratch=(), cost=None, name=None):
    many = isinstance(outputs, (tuple, list))
    inside = pl.BlockSpec(memory_space=pltpu.VMEM)
    held = [
        pltpu.with_memory_space_constraint(value, space) if space == pltpu.HBM else value
        for value, space in zip(inputs, spaces)
    ]
    return pl.pallas_call(
        body,
        out_shape=outputs,
        in_specs=[pl.BlockSpec(memory_space=space) for space in spaces],
        out_specs=[inside] * len(outputs) if many else inside,
        scratch_shapes=list(scratch),
        compiler_params=pltpu.CompilerParams(vmem_limit_bytes=20 << 20),
        cost_estimate=cost,
        name=name,
    )(*held)


def packed(first, second):
    return first[:, :128], second[:, :128], jnp.concatenate([first[:, 128:], second[:, 128:]], axis=1)


def unpacked(wire, spot):
    half = wire.shape[-1] // 2
    rest = wire[spot // 2, 2]
    rest = rest[:, half:] if spot % 2 else rest[:, :half]
    return jnp.concatenate([wire[spot // 2, spot % 2], rest], axis=1)


def send_pairs(send, values):
    for pair in range(len(values) // 2):
        for part, value in enumerate(packed(values[2 * pair], values[2 * pair + 1])):
            send[pair, part] = value


def x_side(got_a, got_b, y, even):
    from_a, from_b = unpacked(got_a, y), unpacked(got_b, y)
    return jnp.where(even, from_b, from_a), jnp.where(even, from_a, from_b)


def strips_kernel(slots_ref, got_a, got_b, send_a, send_b):
    tile_x, tile_y = slots_ref.shape[:2]
    _, even_x = place("gx")
    _, even_y = place("gy")
    first = x_side(got_a, got_b, 0, even_x)
    last = x_side(got_a, got_b, tile_y - 1, even_x)
    for send, upper in ((send_a, even_y), (send_b, jnp.logical_not(even_y))):
        column = jnp.where(upper, tile_y - 1, 0)
        ends = [jnp.where(upper, high, low) for low, high in zip(first, last)]
        middle = [slots_ref[x, column] for x in range(tile_x)]
        send_pairs(send, [ends[0], *middle, ends[1]])


def slot_rows(p_row, m, y, code, pad):
    marks = jnp.where(pad == code, 1.0, 0.0).astype(jnp.bfloat16)
    return jnp.concatenate([p_row[:, y, :], marks], axis=0)


def pad_rows(unknowns, edges):
    return lax.broadcasted_iota(jnp.int32, (ROWS - unknowns, edges), 0) + 1


def edges_kernel(codes_hbm, p_hbm, send_a, send_b, codes, p_ref, arrived):
    tile_x, slots, unknowns, tile_y, edges = p_hbm.shape
    _, even = place("gx")
    rows = (jnp.where(even, tile_x - 1, 0), jnp.where(even, 0, tile_x - 1))
    copies = [pltpu.make_async_copy(codes_hbm, codes, arrived.at[2])]
    for i, row in enumerate(rows):
        copies.append(pltpu.make_async_copy(p_hbm.at[row], p_ref.at[i], arrived.at[i]))
    for copy in copies:
        copy.start()
    for copy in copies:
        copy.wait()
    pad = pad_rows(unknowns, edges)
    for i, (send, row) in enumerate(zip((send_a, send_b), rows)):
        values = [[] for _ in range(tile_y)]
        for m in range(slots):
            p_row = p_ref[i, m]
            for y in range(tile_y):
                values[y].append(slot_rows(p_row, m, y, codes[m, y, row], pad))
        send_pairs(send, [jnp.concatenate(value, axis=0) for value in values])


def start_rows(a_hbm, a_ref, arrived, first):
    copies = {}
    for x in range(a_ref.shape[0]):
        for y in range(a_ref.shape[1]):
            copies[x, y] = pltpu.make_async_copy(
                a_hbm.at[first + x, y], a_ref.at[x, y], arrived.at[x, y]
            )
            copies[x, y].start()
    return copies


def finish_rows(copies, slots_ref, a_ref, result, first):
    for (x, y), copy in copies.items():
        copy.wait()
        for k in range(a_ref.shape[2]):
            result[x, y, k] = jnp.dot(
                slots_ref[first + x, y], a_ref[x, y, k], preferred_element_type=jnp.float32
            ).astype(result.dtype)


def inner_kernel(codes_hbm, p_hbm, a_hbm, slots_ref, faces, result, codes, p_ref, a_ref, arrived, rows_arrived):
    tile_x, slots, unknowns, tile_y, edges = p_ref.shape
    copies = [
        pltpu.make_async_copy(codes_hbm, codes, arrived.at[0]),
        pltpu.make_async_copy(p_hbm, p_ref, arrived.at[1]),
    ]
    for copy in copies:
        copy.start()
    row_copies = start_rows(a_hbm, a_ref, rows_arrived, 0)
    faces[...] = jnp.zeros_like(faces)
    for copy in copies:
        copy.wait()
    pad = pad_rows(unknowns, edges)
    for x in range(tile_x):
        for m in range(slots):
            p_row = p_ref[x, m]
            for y in range(tile_y):
                code = codes[m, y, x]
                block = slot_rows(p_row, m, y, code, pad)
                faces[x, y, code] = block
                slots_ref[x, y, m * ROWS : (m + 1) * ROWS, :] = block
    finish_rows(row_copies, slots_ref, a_ref, result, 0)


def outer_kernel(count_x, unknowns):
    def body(slots_ref, got_xa, got_xb, a_hbm, result, sides, a_ref, rows_arrived):
        first = a_hbm.shape[0] - a_ref.shape[0]
        row_copies = start_rows(a_hbm, a_ref, rows_arrived, first)
        index, even = place("gx")
        for y in range(sides.shape[1]):
            low, high = x_side(got_xa, got_xb, y, even)
            expand(sides.at[0, y], low, index > 0, unknowns)
            expand(sides.at[1, y], high, index < count_x - 1, unknowns)
        finish_rows(row_copies, slots_ref, a_ref, result, first)

    return body


def expand(target, value, live, unknowns):
    edges = value.shape[1]
    value = jnp.where(live, value, jnp.zeros_like(value))
    target[0:ROWS, :] = value[0:ROWS]
    for q in range(1, 5):
        block = None
        for m in range(1, value.shape[0] // ROWS):
            mark = value[m * ROWS + unknowns + q - 1 : m * ROWS + unknowns + q]
            term = mark * value[m * ROWS : (m + 1) * ROWS]
            block = term if block is None else block + term
        target[q * ROWS : (q + 1) * ROWS, :] = block


def face_of(step):
    return face_steps.index(step) if step in face_steps else None


def terms_kernel(count_x, count_y, unknowns):
    span = 49 * unknowns
    lanes = -(-span // 128) * 128

    def body(
        a_hbm, p_hbm, u_first, u_last, faces, sides, got_ya, got_yb,
        own, send_xa, send_xb, send_ya, send_yb,
        a_codes, p_codes, slot_of, part_of, near, products, spread, parts, arrived,
    ):
        tile_x, tile_y = faces.shape[:2]
        slots, held, edges = u_first.shape[2:]
        half = u_first.shape[0]
        mine = [(x, y) for x in range(tile_x) for y in range(tile_y)]
        copies = [
            pltpu.make_async_copy(a_hbm, a_codes, arrived.at[0]),
            pltpu.make_async_copy(p_hbm, p_codes, arrived.at[1]),
        ]
        for copy in copies:
            copy.start()
        index_x, even_x = place("gx")
        index_y, even_y = place("gy")
        wide = tile_y + 2
        flat = near.shape[1:]
        count = held // ROWS
        for i in range(len(mine)):
            for d in range(9):
                slot_of[i, d] = slots
            for q in range(5):
                part_of[i, q] = len(mine) * count
            products[i, slots] = jnp.zeros(products.shape[2:], products.dtype)
        parts[len(mine) * count] = jnp.zeros(parts.shape[1:], parts.dtype)
        for y in range(tile_y):
            near[1 + y] = sides[0, y]
            near[(tile_x + 1) * wide + 1 + y] = sides[1, y]
            for x in range(tile_x):
                near[(1 + x) * wide + 1 + y] = faces[x, y, 0:5].reshape(flat)
        for x in range(tile_x + 2):
            from_a, from_b = unpacked(got_ya, x), unpacked(got_yb, x)
            low, high = index_y > 0, index_y < count_y - 1
            if x == 0:
                low, high = jnp.logical_and(low, index_x > 0), jnp.logical_and(high, index_x > 0)
            if x == tile_x + 1:
                inside = index_x < count_x - 1
                low, high = jnp.logical_and(low, inside), jnp.logical_and(high, inside)
            expand(near.at[x * wide], jnp.where(even_y, from_b, from_a), low, unknowns)
            expand(near.at[x * wide + wide - 1], jnp.where(even_y, from_a, from_b), high, unknowns)
        row = lax.broadcasted_iota(jnp.int32, (held, 128), 0)
        lane = lax.broadcasted_iota(jnp.int32, (held, 128), 1)
        picks = jnp.where(jnp.logical_or(lane == row, lane == row + 64), 1.0, 0.0)
        picks = picks.astype(jnp.bfloat16)
        wing = lax.broadcasted_iota(jnp.int32, (ROWS, 128), 1) < 64
        spread[...] = jnp.zeros_like(spread)
        for copy in copies:
            copy.wait()
        for i, (x, y) in enumerate(mine):
            for k in range(slots):
                slot_of[i, a_codes[x, y, k]] = k
            for m in range(1, count):
                part_of[i, p_codes[m, y, x]] = i * count + m
        gap = jnp.zeros((64 - held, edges), u_first.dtype)
        for k in range(slots):
            for i, (x, y) in enumerate(mine):
                code = jnp.minimum(a_codes[x, y, k], 8) if k else 4
                spot = (x + code // 3) * wide + y + code % 3
                if k:
                    step = lax.div(code, 3)
                    spot = (x + step) * wide + y + code - 3 * step
                one = u_first[x, y, k] if x < half else u_last[x - half, y, k]
                products[i, k] = lax.dot_general(
                    near[spot],
                    jnp.concatenate([one, gap, one, gap], axis=0),
                    NT,
                    preferred_element_type=jnp.float32,
                )
        for i in range(len(mine)):
            stack = spread.at[i % spread.shape[0]]
            found = [slot_of[i, d] if d != 4 else 0 for d in range(9)]
            for o in range(25):
                value = None
                for q, (face_x, face_y) in enumerate(face_steps):
                    step_x, step_y = o // 5 - 2 - face_x, o % 5 - 2 - face_y
                    if abs(step_x) > 1 or abs(step_y) > 1:
                        continue
                    slot = found[3 * step_x + step_y + 4]
                    term = products[i, slot, q * ROWS : (q + 1) * ROWS, :]
                    value = term if value is None else value + term
                if value is None:
                    continue
                high = value.astype(jnp.bfloat16).astype(jnp.float32)
                start = ((o // 5 + 1) * 7 + o % 5 + 1) * unknowns
                stack[start : start + unknowns, :] = jnp.where(wing, high, value - high)[:unknowns]
            terms = lax.dot_general(
                picks, stack[...].astype(jnp.bfloat16), NT, preferred_element_type=jnp.float32
            )
            for m in range(count):
                parts[i * count + m] = terms[m * ROWS : (m + 1) * ROWS]

        def part(x, y, q):
            shift = (face_steps[q][0] * 7 + face_steps[q][1]) * unknowns
            return pltpu.roll(parts[part_of[x * tile_y + y, q]], (-shift) % lanes, 1)

        for i, (x, y) in enumerate(mine):
            value = parts[i * count]
            for q in range(1, 5):
                from_x, from_y = x - face_steps[q][0], y - face_steps[q][1]
                if 0 <= from_x < tile_x and 0 <= from_y < tile_y:
                    value += part(from_x, from_y, q)
            own[x, y] = value[0:unknowns, 0:span]
        for y in range(tile_y):
            low, high = part(0, y, 1), part(tile_x - 1, y, 2)
            send_xa[y] = jnp.where(even_x, high, low).astype(send_xa.dtype)
            send_xb[y] = jnp.where(even_x, low, high).astype(send_xb.dtype)
        for x in range(tile_x):
            low, high = part(x, 0, 3), part(x, tile_y - 1, 4)
            send_ya[x] = jnp.where(even_y, high, low).astype(send_ya.dtype)
            send_yb[x] = jnp.where(even_y, low, high).astype(send_yb.dtype)

    return body


def sum_kernel(count_x, count_y):
    def body(own, got_xa, got_xb, got_ya, got_yb, result):
        tile_x, tile_y, unknowns, span = own.shape
        index_x, even_x = place("gx")
        index_y, even_y = place("gy")

        def shown(value, live):
            value = value[0:unknowns, 0:span].astype(jnp.float32)
            return jnp.where(live, value, jnp.zeros_like(value))

        low_x, high_x = index_x > 0, index_x < count_x - 1
        low_y, high_y = index_y > 0, index_y < count_y - 1
        for x in range(tile_x):
            for y in range(tile_y):
                value = own[x, y]
                if x == 0:
                    value += shown(jnp.where(even_x, got_xb[y], got_xa[y]), low_x)
                if x == tile_x - 1:
                    value += shown(jnp.where(even_x, got_xa[y], got_xb[y]), high_x)
                if y == 0:
                    value += shown(jnp.where(even_y, got_yb[x], got_ya[x]), low_y)
                if y == tile_y - 1:
                    value += shown(jnp.where(even_y, got_ya[x], got_yb[x]), high_y)
                result[x, :, y, :] = value

    return body


def solution(mesh):
    count_x, count_y = mesh.shape["gx"], mesh.shape["gy"]
    pairs = exchange_pairs(count_x, count_y)
    hbm, inside = pltpu.HBM, pltpu.VMEM

    def shards(a_blocks, a_codes, p_blocks, p_codes):
        tile_x, tile_y, slots, edges, _ = a_blocks.shape
        held, unknowns = p_blocks.shape[2:4]
        span = 49 * unknowns
        lanes = -(-span // 128) * 128
        half = lambda *dims: jax.ShapeDtypeStruct(dims, jnp.bfloat16)
        codes = jnp.transpose(p_codes, (2, 1, 0))
        blocks = jnp.transpose(p_blocks, (0, 2, 3, 1, 4))
        wire = (3, held * ROWS, 128)
        dma = pltpu.SemaphoreType.DMA
        send_a, send_b = run(
            edges_kernel,
            (codes, blocks),
            (hbm, hbm),
            (half(tile_y // 2, *wire), half(tile_y // 2, *wire)),
            scratch=(
                pltpu.SMEM(codes.shape, codes.dtype),
                pltpu.VMEM((2, *blocks.shape[1:]), blocks.dtype),
                dma((3,)),
            ),
            name="edges",
        )
        got_xa = lax.ppermute(send_a, AXES, pairs[0])
        got_xb = lax.ppermute(send_b, AXES, pairs[1])
        early = tile_x // 2
        late = tile_x - early
        row_cost = lambda rows: pl.CostEstimate(
            flops=2 * held * ROWS * rows * (a_blocks.size // tile_x),
            bytes_accessed=2 * rows * (a_blocks.size // tile_x),
            transcendentals=0,
        )
        slots_ref, faces, u_first = run(
            inner_kernel,
            (codes, blocks, a_blocks),
            (hbm, hbm, hbm),
            (
                half(tile_x, tile_y, held * ROWS, edges),
                half(tile_x, tile_y, 6, ROWS, edges),
                half(early, tile_y, slots, held * ROWS, edges),
            ),
            scratch=(
                pltpu.SMEM(codes.shape, codes.dtype),
                pltpu.VMEM(blocks.shape, blocks.dtype),
                pltpu.VMEM((early, *a_blocks.shape[1:]), a_blocks.dtype),
                dma((2,)),
                dma((early, tile_y)),
            ),
            cost=row_cost(early),
            name="inner",
        )
        send_a, send_b = run(
            strips_kernel,
            (slots_ref, got_xa, got_xb),
            (inside,) * 3,
            (half(tile_x // 2 + 1, *wire), half(tile_x // 2 + 1, *wire)),
            name="strips",
        )
        got_ya = lax.ppermute(send_a, AXES, pairs[2])
        got_yb = lax.ppermute(send_b, AXES, pairs[3])
        u_last, sides = run(
            outer_kernel(count_x, unknowns),
            (slots_ref, got_xa, got_xb, a_blocks),
            (inside, inside, inside, hbm),
            (
                half(late, tile_y, slots, held * ROWS, edges),
                half(2, tile_y, 5 * ROWS, edges),
            ),
            scratch=(
                pltpu.VMEM((late, *a_blocks.shape[1:]), a_blocks.dtype),
                dma((late, tile_y)),
            ),
            cost=row_cost(late),
            name="outer",
        )
        amount = tile_x * tile_y
        own, *sends = run(
            terms_kernel(count_x, count_y, unknowns),
            (a_codes, codes, u_first, u_last, faces, sides, got_ya, got_yb),
            (hbm, hbm) + (inside,) * 6,
            (
                jax.ShapeDtypeStruct((tile_x, tile_y, unknowns, span), jnp.float32),
                half(tile_y, ROWS, lanes),
                half(tile_y, ROWS, lanes),
                half(tile_x, ROWS, lanes),
                half(tile_x, ROWS, lanes),
            ),
            scratch=(
                pltpu.SMEM(a_codes.shape, a_codes.dtype),
                pltpu.SMEM(codes.shape, codes.dtype),
                pltpu.SMEM((amount, 10), jnp.int32),
                pltpu.SMEM((amount, 6), jnp.int32),
                pltpu.VMEM(((tile_x + 2) * (tile_y + 2), 5 * ROWS, edges), jnp.bfloat16),
                pltpu.VMEM((amount, slots + 1, 5 * ROWS, 128), jnp.float32),
                pltpu.VMEM((4, lanes, 128), jnp.float32),
                pltpu.VMEM((amount * held + 1, ROWS, lanes), jnp.float32),
                dma((2,)),
            ),
            name="terms",
        )
        got = [lax.ppermute(send, AXES, p) for send, p in zip(sends, pairs)]
        result = run(
            sum_kernel(count_x, count_y),
            (own, *got),
            (inside,) * 5,
            jax.ShapeDtypeStruct((tile_x, unknowns, tile_y, span), jnp.float32),
            name="sum",
        )
        return jnp.transpose(result, (0, 2, 1, 3))

    in_specs = (
        P("gx", "gy", None, None, None),
        P("gx", "gy", None),
        P("gx", "gy", None, None, None),
        P("gx", "gy", None),
    )
    out_specs = P("gx", "gy", None, None)
    return jax.shard_map(shards, mesh=mesh, in_specs=in_specs, out_specs=out_specs, check_vma=False)
```

```python
import jax
import jax.numpy as jnp
from jax import lax
from jax.experimental import pallas as pl
from jax.experimental.pallas import tpu as pltpu
from jax.sharding import PartitionSpec as P

face_steps = ((0, 0), (-1, 0), (1, 0), (0, -1), (0, 1))
ROWS = 16
NT = (((1,), (1,)), ((), ()))
AXES = ("gx", "gy")


def exchange_pairs(count_x, count_y):
    spot = lambda x, y: x * count_y + y
    result = []
    for parity in (0, 1):
        pairs = []
        for x in range(count_x):
            other = x + 1 if (x % 2 == parity) else x - 1
            for y in range(count_y):
                inside = 0 <= other < count_x
                pairs.append((spot(x, y), spot(other, y) if inside else spot(x, y ^ 1)))
        result.append(pairs)
    for parity in (0, 1):
        pairs = []
        for y in range(count_y):
            other = y + 1 if (y % 2 == parity) else y - 1
            for x in range(count_x):
                inside = 0 <= other < count_y
                pairs.append((spot(x, y), spot(x, other) if inside else spot(x ^ 1, y)))
        result.append(pairs)
    return result


def place(axis):
    index = lax.axis_index(axis)
    even = lax.rem(index, 2) == 0
    return index, even


def run(body, inputs, spaces, outputs, scratch=(), cost=None, name=None):
    many = isinstance(outputs, (tuple, list))
    inside = pl.BlockSpec(memory_space=pltpu.VMEM)
    held = [
        pltpu.with_memory_space_constraint(value, space) if space == pltpu.HBM else value
        for value, space in zip(inputs, spaces)
    ]
    return pl.pallas_call(
        body,
        out_shape=outputs,
        in_specs=[pl.BlockSpec(memory_space=space) for space in spaces],
        out_specs=[inside] * len(outputs) if many else inside,
        scratch_shapes=list(scratch),
        compiler_params=pltpu.CompilerParams(vmem_limit_bytes=20 << 20),
        cost_estimate=cost,
        name=name,
    )(*held)


def packed(first, second):
    return first[:, :128], second[:, :128], jnp.concatenate([first[:, 128:], second[:, 128:]], axis=1)


def unpacked(wire, spot):
    half = wire.shape[-1] // 2
    rest = wire[spot // 2, 2]
    rest = rest[:, half:] if spot % 2 else rest[:, :half]
    return jnp.concatenate([wire[spot // 2, spot % 2], rest], axis=1)


def send_pairs(send, values):
    for pair in range(len(values) // 2):
        for part, value in enumerate(packed(values[2 * pair], values[2 * pair + 1])):
            send[pair, part] = value


def x_side(got_a, got_b, y, even):
    from_a, from_b = unpacked(got_a, y), unpacked(got_b, y)
    return jnp.where(even, from_b, from_a), jnp.where(even, from_a, from_b)


def strips_kernel(slots_ref, got_a, got_b, send_a, send_b):
    tile_x, tile_y = slots_ref.shape[:2]
    _, even_x = place("gx")
    _, even_y = place("gy")
    first = x_side(got_a, got_b, 0, even_x)
    last = x_side(got_a, got_b, tile_y - 1, even_x)
    for send, upper in ((send_a, even_y), (send_b, jnp.logical_not(even_y))):
        column = jnp.where(upper, tile_y - 1, 0)
        ends = [jnp.where(upper, high, low) for low, high in zip(first, last)]
        middle = [slots_ref[x, column] for x in range(tile_x)]
        send_pairs(send, [ends[0], *middle, ends[1]])


def slot_rows(p_row, m, y, code, pad):
    marks = jnp.where(pad == code, 1.0, 0.0).astype(jnp.bfloat16)
    return jnp.concatenate([p_row[:, y, :], marks], axis=0)


def pad_rows(unknowns, edges):
    return lax.broadcasted_iota(jnp.int32, (ROWS - unknowns, edges), 0) + 1


def edges_kernel(codes_hbm, p_hbm, send_a, send_b, codes, p_ref, arrived):
    tile_x, slots, unknowns, tile_y, edges = p_hbm.shape
    _, even = place("gx")
    rows = (jnp.where(even, tile_x - 1, 0), jnp.where(even, 0, tile_x - 1))
    copies = [pltpu.make_async_copy(codes_hbm, codes, arrived.at[2])]
    for i, row in enumerate(rows):
        copies.append(pltpu.make_async_copy(p_hbm.at[row], p_ref.at[i], arrived.at[i]))
    for copy in copies:
        copy.start()
    for copy in copies:
        copy.wait()
    pad = pad_rows(unknowns, edges)
    for i, (send, row) in enumerate(zip((send_a, send_b), rows)):
        values = [[] for _ in range(tile_y)]
        for m in range(slots):
            p_row = p_ref[i, m]
            for y in range(tile_y):
                values[y].append(slot_rows(p_row, m, y, codes[m, y, row], pad))
        send_pairs(send, [jnp.concatenate(value, axis=0) for value in values])


def start_rows(a_hbm, a_ref, arrived, first):
    copies = []
    for x in range(a_ref.shape[0]):
        copies.append(pltpu.make_async_copy(a_hbm.at[first + x], a_ref.at[x], arrived.at[x]))
        copies[x].start()
    return copies


def finish_rows(copies, slots_ref, a_ref, result, first):
    for x, copy in enumerate(copies):
        copy.wait()
        for y in range(a_ref.shape[1]):
            for k in range(a_ref.shape[2]):
                result[x, y, k] = jnp.dot(
                    slots_ref[first + x, y], a_ref[x, y, k], preferred_element_type=jnp.float32
                ).astype(result.dtype)


def inner_kernel(codes_hbm, p_hbm, a_hbm, slots_ref, result, codes, p_ref, a_ref, arrived, rows_arrived):
    tile_x, slots, unknowns, tile_y, edges = p_ref.shape
    copies = [
        pltpu.make_async_copy(codes_hbm, codes, arrived.at[0]),
        pltpu.make_async_copy(p_hbm, p_ref, arrived.at[1]),
    ]
    for copy in copies:
        copy.start()
    row_copies = start_rows(a_hbm, a_ref, rows_arrived, 0)
    for copy in copies:
        copy.wait()
    pad = pad_rows(unknowns, edges)
    for x in range(tile_x):
        for m in range(slots):
            p_row = p_ref[x, m]
            for y in range(tile_y):
                slots_ref[x, y, m * ROWS : (m + 1) * ROWS, :] = slot_rows(
                    p_row, m, y, codes[m, y, x], pad
                )
    finish_rows(row_copies, slots_ref, a_ref, result, 0)


def outer_kernel(count_x, unknowns):
    def body(
        slots_ref, got_xa, got_xb, codes_hbm, a_hbm,
        result, sides, faces, codes, a_ref, arrived, rows_arrived,
    ):
        copy = pltpu.make_async_copy(codes_hbm, codes, arrived.at[0])
        copy.start()
        first = a_hbm.shape[0] - a_ref.shape[0]
        row_copies = start_rows(a_hbm, a_ref, rows_arrived, first)
        index, even = place("gx")
        for y in range(sides.shape[1]):
            low, high = x_side(got_xa, got_xb, y, even)
            expand(sides.at[0, y], low, index > 0, unknowns)
            expand(sides.at[1, y], high, index < count_x - 1, unknowns)
        faces[...] = jnp.zeros_like(faces)
        copy.wait()
        for x in range(faces.shape[0]):
            for y in range(faces.shape[1]):
                for m in range(codes.shape[0]):
                    block = slots_ref[x, y, m * ROWS : (m + 1) * ROWS, :]
                    faces[x, y, codes[m, y, x]] = block
        finish_rows(row_copies, slots_ref, a_ref, result, first)

    return body


def expand(target, value, live, unknowns):
    edges = value.shape[1]
    value = jnp.where(live, value, jnp.zeros_like(value))
    target[0:ROWS, :] = value[0:ROWS]
    for q in range(1, 5):
        block = None
        for m in range(1, value.shape[0] // ROWS):
            mark = value[m * ROWS + unknowns + q - 1 : m * ROWS + unknowns + q]
            term = mark * value[m * ROWS : (m + 1) * ROWS]
            block = term if block is None else block + term
        target[q * ROWS : (q + 1) * ROWS, :] = block


def face_of(step):
    return face_steps.index(step) if step in face_steps else None


def terms_kernel(count_x, count_y, unknowns):
    span = 49 * unknowns
    lanes = -(-span // 128) * 128

    def body(
        a_hbm, p_hbm, u_first, u_last, faces, sides, got_ya, got_yb,
        parts, send_xa, send_xb, send_ya, send_yb,
        a_codes, p_codes, slot_of, part_of, near, products, spread, arrived,
    ):
        tile_x, tile_y = faces.shape[:2]
        slots, held, edges = u_first.shape[2:]
        half = u_first.shape[0]
        mine = [(x, y) for x in range(tile_x) for y in range(tile_y)]
        copies = [
            pltpu.make_async_copy(a_hbm, a_codes, arrived.at[0]),
            pltpu.make_async_copy(p_hbm, p_codes, arrived.at[1]),
        ]
        for copy in copies:
            copy.start()
        index_x, even_x = place("gx")
        index_y, even_y = place("gy")
        wide = tile_y + 2
        flat = near.shape[1:]
        count = held // ROWS
        for i in range(len(mine)):
            for d in range(9):
                slot_of[i, d] = len(mine) * slots
            for q in range(5):
                part_of[i, q] = len(mine) * count
        products[len(mine) * slots] = jnp.zeros(products.shape[1:], products.dtype)
        parts[len(mine) * count] = jnp.zeros(parts.shape[1:], parts.dtype)
        for y in range(tile_y):
            near[1 + y] = sides[0, y]
            near[(tile_x + 1) * wide + 1 + y] = sides[1, y]
            for x in range(tile_x):
                near[(1 + x) * wide + 1 + y] = faces[x, y, 0:5].reshape(flat)
        for x in range(tile_x + 2):
            from_a, from_b = unpacked(got_ya, x), unpacked(got_yb, x)
            low, high = index_y > 0, index_y < count_y - 1
            if x == 0:
                low, high = jnp.logical_and(low, index_x > 0), jnp.logical_and(high, index_x > 0)
            if x == tile_x + 1:
                inside = index_x < count_x - 1
                low, high = jnp.logical_and(low, inside), jnp.logical_and(high, inside)
            expand(near.at[x * wide], jnp.where(even_y, from_b, from_a), low, unknowns)
            expand(near.at[x * wide + wide - 1], jnp.where(even_y, from_a, from_b), high, unknowns)
        for o in reversed(range(26)):
            start = ((o // 5 + 1) * 7 + o % 5 + 1) * unknowns if o < 25 else lanes
            ended = ((o - 1) // 5 * 7 + 7 + (o - 1) % 5 + 2) * unknowns if o else 0
            if start > ended:
                zeros = jnp.zeros((start - ended, spread.shape[2]), spread.dtype)
                for i in range(spread.shape[0]):
                    spread[i, ended:start, :] = zeros
        for copy in copies:
            copy.wait()
        for i, (x, y) in enumerate(mine):
            for k in range(slots):
                slot_of[i, a_codes[x, y, k]] = i * slots + k
            for m in range(1, count):
                part_of[i, p_codes[m, y, x]] = i * count + m
        for k in range(slots):
            for i, (x, y) in enumerate(mine):
                code = jnp.minimum(a_codes[x, y, k], 8) if k else 4
                spot = (x + code // 3) * wide + y + code % 3
                if k:
                    step = lax.div(code, 3)
                    spot = (x + step) * wide + y + code - 3 * step
                one = u_first[x, y, k] if x < half else u_last[x - half, y, k]
                products[i * slots + k] = lax.dot_general(
                    near[spot], one, NT, preferred_element_type=jnp.float32
                )
        for i in range(len(mine)):
            stack = spread.at[i % spread.shape[0]]
            found = [slot_of[i, d] if d != 4 else i * slots for d in range(9)]
            for o in range(25):
                value = None
                for q, (face_x, face_y) in enumerate(face_steps):
                    step_x, step_y = o // 5 - 2 - face_x, o % 5 - 2 - face_y
                    if abs(step_x) > 1 or abs(step_y) > 1:
                        continue
                    slot = found[3 * step_x + step_y + 4]
                    term = products[slot, q * ROWS : (q + 1) * ROWS, :]
                    value = term if value is None else value + term
                start = ((o // 5 + 1) * 7 + o % 5 + 1) * unknowns
                if value is None:
                    value = jnp.zeros((ROWS, held), jnp.float32)
                stack[start : start + unknowns, :] = value[:unknowns]
            terms = jnp.transpose(stack[...])
            for m in range(count):
                parts[i * count + m] = terms[m * ROWS : (m + 1) * ROWS]

        part = part_reader(parts, part_of, tile_y, unknowns)
        for y in range(tile_y):
            low, high = part(0, y, 1), part(tile_x - 1, y, 2)
            send_xa[y] = jnp.where(even_x, high, low).astype(send_xa.dtype)
            send_xb[y] = jnp.where(even_x, low, high).astype(send_xb.dtype)
        for x in range(tile_x):
            low, high = part(x, 0, 3), part(x, tile_y - 1, 4)
            send_ya[x] = jnp.where(even_y, high, low).astype(send_ya.dtype)
            send_yb[x] = jnp.where(even_y, low, high).astype(send_yb.dtype)

    return body


def part_reader(parts, part_of, tile_y, unknowns):
    lanes = parts.shape[2]

    def part(x, y, q):
        shift = (face_steps[q][0] * 7 + face_steps[q][1]) * unknowns
        return pltpu.roll(parts[part_of[x * tile_y + y, q]], (-shift) % lanes, 1)

    return part


def own_kernel(p_hbm, parts, own, p_codes, part_of, arrived):
    tile_x, tile_y, unknowns, span = own.shape
    copy = pltpu.make_async_copy(p_hbm, p_codes, arrived.at[0])
    copy.start()
    count = p_codes.shape[0]
    amount = tile_x * tile_y
    for i in range(amount):
        for q in range(5):
            part_of[i, q] = amount * count
    copy.wait()
    for x in range(tile_x):
        for y in range(tile_y):
            i = x * tile_y + y
            for m in range(1, count):
                part_of[i, p_codes[m, y, x]] = i * count + m
    part = part_reader(parts, part_of, tile_y, unknowns)
    for x in range(tile_x):
        for y in range(tile_y):
            value = parts[(x * tile_y + y) * count]
            for q in range(1, 5):
                from_x, from_y = x - face_steps[q][0], y - face_steps[q][1]
                if 0 <= from_x < tile_x and 0 <= from_y < tile_y:
                    value += part(from_x, from_y, q)
            own[x, y] = value[0:unknowns, 0:span]


def sum_kernel(count_x, count_y):
    def body(own, got_xa, got_xb, got_ya, got_yb, result):
        tile_x, tile_y, unknowns, span = own.shape
        index_x, even_x = place("gx")
        index_y, even_y = place("gy")

        def shown(value, live):
            value = value[0:unknowns, 0:span].astype(jnp.float32)
            return jnp.where(live, value, jnp.zeros_like(value))

        low_x, high_x = index_x > 0, index_x < count_x - 1
        low_y, high_y = index_y > 0, index_y < count_y - 1
        for x in range(tile_x):
            for y in range(tile_y):
                value = own[x, y]
                if x == 0:
                    value += shown(jnp.where(even_x, got_xb[y], got_xa[y]), low_x)
                if x == tile_x - 1:
                    value += shown(jnp.where(even_x, got_xa[y], got_xb[y]), high_x)
                if y == 0:
                    value += shown(jnp.where(even_y, got_yb[x], got_ya[x]), low_y)
                if y == tile_y - 1:
                    value += shown(jnp.where(even_y, got_ya[x], got_yb[x]), high_y)
                result[x, :, y, :] = value

    return body


def solution(mesh):
    count_x, count_y = mesh.shape["gx"], mesh.shape["gy"]
    pairs = exchange_pairs(count_x, count_y)
    hbm, inside = pltpu.HBM, pltpu.VMEM

    def shards(a_blocks, a_codes, p_blocks, p_codes):
        tile_x, tile_y, slots, edges, _ = a_blocks.shape
        held, unknowns = p_blocks.shape[2:4]
        span = 49 * unknowns
        lanes = -(-span // 128) * 128
        half = lambda *dims: jax.ShapeDtypeStruct(dims, jnp.bfloat16)
        codes = jnp.transpose(p_codes, (2, 1, 0))
        blocks = jnp.transpose(p_blocks, (0, 2, 3, 1, 4))
        wire = (3, held * ROWS, 128)
        dma = pltpu.SemaphoreType.DMA
        send_a, send_b = run(
            edges_kernel,
            (codes, blocks),
            (hbm, hbm),
            (half(tile_y // 2, *wire), half(tile_y // 2, *wire)),
            scratch=(
                pltpu.SMEM(codes.shape, codes.dtype),
                pltpu.VMEM((2, *blocks.shape[1:]), blocks.dtype),
                dma((3,)),
            ),
            name="edges",
        )
        got_xa = lax.ppermute(send_a, AXES, pairs[0])
        got_xb = lax.ppermute(send_b, AXES, pairs[1])
        early = tile_x // 2
        late = tile_x - early
        row_cost = lambda rows: pl.CostEstimate(
            flops=2 * held * ROWS * rows * (a_blocks.size // tile_x),
            bytes_accessed=2 * rows * (a_blocks.size // tile_x),
            transcendentals=0,
        )
        slots_ref, u_first = run(
            inner_kernel,
            (codes, blocks, a_blocks),
            (hbm, hbm, hbm),
            (
                half(tile_x, tile_y, held * ROWS, edges),
                half(early, tile_y, slots, held * ROWS, edges),
            ),
            scratch=(
                pltpu.SMEM(codes.shape, codes.dtype),
                pltpu.VMEM(blocks.shape, blocks.dtype),
                pltpu.VMEM((early, *a_blocks.shape[1:]), a_blocks.dtype),
                dma((2,)),
                dma((early,)),
            ),
            cost=row_cost(early),
            name="inner",
        )
        send_a, send_b = run(
            strips_kernel,
            (slots_ref, got_xa, got_xb),
            (inside,) * 3,
            (half(tile_x // 2 + 1, *wire), half(tile_x // 2 + 1, *wire)),
            name="strips",
        )
        got_ya = lax.ppermute(send_a, AXES, pairs[2])
        got_yb = lax.ppermute(send_b, AXES, pairs[3])
        u_last, sides, faces = run(
            outer_kernel(count_x, unknowns),
            (slots_ref, got_xa, got_xb, codes, a_blocks),
            (inside, inside, inside, hbm, hbm),
            (
                half(late, tile_y, slots, held * ROWS, edges),
                half(2, tile_y, 5 * ROWS, edges),
                half(tile_x, tile_y, 6, ROWS, edges),
            ),
            scratch=(
                pltpu.SMEM(codes.shape, codes.dtype),
                pltpu.VMEM((late, *a_blocks.shape[1:]), a_blocks.dtype),
                dma((1,)),
                dma((late,)),
            ),
            cost=row_cost(late),
            name="outer",
        )
        amount = tile_x * tile_y
        parts, *sends = run(
            terms_kernel(count_x, count_y, unknowns),
            (a_codes, codes, u_first, u_last, faces, sides, got_ya, got_yb),
            (hbm, hbm) + (inside,) * 6,
            (
                jax.ShapeDtypeStruct((amount * held + 1, ROWS, lanes), jnp.float32),
                half(tile_y, ROWS, lanes),
                half(tile_y, ROWS, lanes),
                half(tile_x, ROWS, lanes),
                half(tile_x, ROWS, lanes),
            ),
            scratch=(
                pltpu.SMEM(a_codes.shape, a_codes.dtype),
                pltpu.SMEM(codes.shape, codes.dtype),
                pltpu.SMEM((amount, 10), jnp.int32),
                pltpu.SMEM((amount, 6), jnp.int32),
                pltpu.VMEM(((tile_x + 2) * (tile_y + 2), 5 * ROWS, edges), jnp.bfloat16),
                pltpu.VMEM((amount * slots + 1, 5 * ROWS, held * ROWS), jnp.float32),
                pltpu.VMEM((2, lanes, held * ROWS), jnp.float32),
                dma((2,)),
            ),
            name="terms",
        )
        got = [lax.ppermute(send, AXES, p) for send, p in zip(sends, pairs)]
        own = run(
            own_kernel,
            (codes, parts),
            (hbm, inside),
            jax.ShapeDtypeStruct((tile_x, tile_y, unknowns, span), jnp.float32),
            scratch=(
                pltpu.SMEM(codes.shape, codes.dtype),
                pltpu.SMEM((amount, 6), jnp.int32),
                dma((1,)),
            ),
            cost=pl.CostEstimate(flops=0, bytes_accessed=4 << 20, transcendentals=0),
            name="own",
        )
        result = run(
            sum_kernel(count_x, count_y),
            (own, *got),
            (inside,) * 5,
            jax.ShapeDtypeStruct((tile_x, unknowns, tile_y, span), jnp.float32),
            name="sum",
        )
        return jnp.transpose(result, (0, 2, 1, 3))

    in_specs = (
        P("gx", "gy", None, None, None),
        P("gx", "gy", None),
        P("gx", "gy", None, None, None),
        P("gx", "gy", None),
    )
    out_specs = P("gx", "gy", None, None)
    return jax.shard_map(shards, mesh=mesh, in_specs=in_specs, out_specs=out_specs, check_vma=False)
```
